32 devices in a mesh: tm: 4 (over y, x), inner: 8 (over z, core).
Axes of the slice: x: 2, y: 2, z: 4, core: 2. Of those that a mesh axis runs over, the one named last changes fastest.
Arguments:
- frames: bfloat16 [32, 256, 768], P(('tm', 'inner')), may hold values from -6 to 6
- norm_gain: float32 [768], replicated, may hold values from 0.25 to 1.75
- w_qkv: bfloat16 [768, 2304], replicated, may hold values from -16 to 16
- w_out: bfloat16 [768, 768], replicated, may hold values from -0.21875 to 0.21875
- cotangent: bfloat16 [32, 256, 768], P(('tm', 'inner')), may hold values from -6 to 6
Outputs:
- block_out: bfloat16 [32, 256, 768], P(('tm', 'inner'))
- frames_grad: bfloat16 [32, 256, 768], P(('tm', 'inner'))
- qkv_weight_grad: float32 [768, 2304], P('inner', 'tm')
- out_weight_grad: float32 [768, 768], P('inner', 'tm')
- gain_grad: float32 [768], P('inner')
The draws below stay inside these ranges and needn't reach their ends.
All inputs are finite; a program needn't handle non-finite values.
Results may differ from the reference program's by a relative error of at most 0.012.
The reference program's roundings to bfloat16 on the way (of `normed`, `qkv_rows`, `weights_b`, `mixed_rows`, `grad_mix`, `score_grad` and `qkv_rows_grad`) count: a program that leaves them out, or rounds other values in their place, can miss the bound.
Values may be sent and summed in bfloat16 or wider, within the bound.
No kernel may reach another device: no remote copies, remote signals or barrier semaphores. Data moves between devices by JAX's collectives and lax.ppermute only.
A program may use at most 128 MiB of HBM per device.

```python
import math
import jax
import jax.numpy as jnp
from jax import lax

D = 768
HEADS = 12
HEAD_DIM = 64
P_SIZE = 256
WINDOW = 4
FRAMES = 32
CLIP = 32
TOKENS = 8192


def draw_frames(key, part):
    key_one = jax.random.fold_in(key, 0)
    values = jax.random.normal(key_one, (FRAMES, P_SIZE, D), jnp.float32)
    return jnp.clip(values, -6.0, 6.0).astype(jnp.bfloat16)


def draw_w_qkv(key, part):
    key_one = jax.random.fold_in(key, 0)
    base_w = jnp.clip(jax.random.normal(key_one, (D, 3 * D), jnp.float32), -6.0, 6.0) / math.sqrt(D)
    return jnp.clip(base_w, -16.0, 16.0).astype(jnp.bfloat16)


def strengthened(array, rng, source, target, blocks, factor):
    def block_of(axis_at):
        return (jnp.arange(array.shape[axis_at]) // (array.shape[axis_at] // blocks)).reshape((-1,) + (1,) * (array.ndim - 1 - axis_at))

    first = jax.random.permutation(rng, blocks)[block_of(target)]
    other_side = (block_of(target) + blocks // 2) % blocks
    return jnp.where((block_of(source) == first) | (block_of(source) == other_side), factor * array, array)


def level_of(stream_key, extent, pieces, least, top_value):
    def one(dim, shards_of):
        heights = jax.random.uniform(jax.random.fold_in(jax.random.fold_in(stream_key, 6), dim), (shards_of,), jnp.float32, least / len(pieces), top_value / len(pieces))
        return jnp.repeat(jnp.exp(heights), extent[dim] // shards_of).reshape((-1,) + (1,) * (len(extent) - dim - 1))

    level = one(*pieces[0])
    for cut in pieces[1:]:
        level = level * one(*cut)
    return level


def scatter_about(rng, dims, scale, bound, shards=(), held_as=jnp.bfloat16):
    entries = jax.random.normal(rng, dims, jnp.float32) * scale
    if len(shards) > 0:
        entries = level_of(rng, dims, shards, -0.22, 0.18) * entries
    return jnp.clip(entries, min=-bound, max=bound).astype(held_as)


def noise_with(own_key, extent, scale, bound, shards, heavy, held_as=jnp.bfloat16):
    drawn = scale * jax.random.normal(own_key, extent, jnp.float32)
    if shards:
        drawn = drawn * level_of(own_key, extent, shards, -0.22, 0.18)
    return jnp.clip(strengthened(drawn, jax.random.fold_in(own_key, 3), *heavy), -bound, bound).astype(held_as)


def setup_inputs(seed: int = 0) -> dict:
    key_of = jax.random.split(jax.random.key(seed), 6)
    frames = draw_frames(jax.random.fold_in(key_of[5], 71), 0)
    norm_gain = jnp.clip(1.0 + 0.15 * jax.random.normal(key_of[1], (D,), jnp.float32), 0.25, 1.75)
    w_qkv = draw_w_qkv(jax.random.fold_in(key_of[5], 71), 0)
    w_out = scatter_about(key_of[3], (D, D), D ** -0.5, 0.21875)
    cotangent = noise_with(key_of[4], (FRAMES, P_SIZE, D), 1.0, 6.0, ((0, 32),), (0, 2, 32, 2.75))
    return dict(frames=frames, norm_gain=norm_gain, w_qkv=w_qkv, w_out=w_out, cotangent=cotangent)


EPSILON = 1e-06

def normalize(row_data, norm_gain):
    wide_vals = row_data.astype(jnp.float32)
    center = wide_vals - lax.optimization_barrier(jnp.mean(wide_vals, axis=-1, keepdims=True))
    spread = lax.rsqrt(lax.optimization_barrier(jnp.mean(center * center, axis=-1, keepdims=True)) + EPSILON)
    unit_rows = center * spread
    return ((unit_rows * norm_gain).astype(jnp.bfloat16), unit_rows, spread)

def norm_back(normed_grad, unit_rows, spread, norm_gain):
    scaled = normed_grad * norm_gain
    mean_one = lax.optimization_barrier(jnp.mean(scaled, axis=-1, keepdims=True))
    second = lax.optimization_barrier(jnp.mean(scaled * unit_rows, axis=-1, keepdims=True))
    return spread * (scaled - mean_one - unit_rows * second)

def project(row_data, weight):
    flat_rows = row_data.reshape(-1, row_data.shape[-1])
    result = jnp.dot(flat_rows, weight, preferred_element_type=jnp.float32)
    return result.reshape(row_data.shape[:-1] + (weight.shape[1],))

def project_back(row_data, weight):
    flat_rows = row_data.reshape(-1, row_data.shape[-1])
    result = lax.dot_general(flat_rows, weight, (((1,), (1,)), ((), ())), preferred_element_type=jnp.float32)
    return result.reshape(row_data.shape[:-1] + (weight.shape[0],))

def contract(left_rows, right_rows):
    left_flat = left_rows.reshape(-1, left_rows.shape[-1])
    right_flat = right_rows.reshape(-1, right_rows.shape[-1])
    return lax.dot_general(left_flat, right_flat, (((0,), (0,)), ((), ())), preferred_element_type=jnp.float32)

def heads_of(row_data):
    return row_data.reshape(row_data.shape[:-1] + (HEADS, HEAD_DIM))

def attend(query_rows, key_pad, value_pad, first_frame, all_frames, clip_len):
    held_frames = query_rows.shape[0]
    span_len = 2 * WINDOW + 1
    score_scale = HEAD_DIM ** (-0.5)
    query_h = heads_of(query_rows).astype(jnp.float32)
    score_list = []
    for offset in range(span_len):
        key_h = heads_of(key_pad[offset:offset + held_frames]).astype(jnp.float32)
        score_list.append(jnp.einsum('ftnd,ftnd->ftn', query_h, key_h))
    scores = jnp.stack(score_list) * score_scale
    query_at = first_frame + jnp.arange(held_frames)[None, :]
    frame_at = query_at + jnp.arange(span_len)[:, None] - WINDOW
    inside = (frame_at >= 0) & (frame_at < all_frames) & (frame_at // clip_len == query_at // clip_len)
    inside = inside[:, :, None, None]
    scores = jnp.where(inside, scores, -1e+30)
    row_top = lax.optimization_barrier(jnp.max(scores, axis=0, keepdims=True))
    exp_scores = jnp.exp(scores - row_top)
    soft_probs = exp_scores / lax.optimization_barrier(jnp.sum(exp_scores, axis=0, keepdims=True))
    weights_b = soft_probs.astype(jnp.bfloat16)
    mixed_rows = jnp.zeros(query_h.shape, jnp.float32)
    for offset in range(span_len):
        value_h = heads_of(value_pad[offset:offset + held_frames]).astype(jnp.float32)
        mixed_rows = mixed_rows + weights_b[offset][..., None].astype(jnp.float32) * value_h
    mixed_rows = mixed_rows.reshape(query_rows.shape).astype(jnp.bfloat16)
    return (mixed_rows, soft_probs, weights_b)

def attend_back(query_rows, key_pad, value_pad, soft_probs, weights_b, grad_mix):
    held_frames = query_rows.shape[0]
    span_len = 2 * WINDOW + 1
    score_scale = HEAD_DIM ** (-0.5)
    query_h = heads_of(query_rows).astype(jnp.float32)
    grad_h = heads_of(grad_mix).astype(jnp.float32)
    dot_list = []
    for offset in range(span_len):
        value_h = heads_of(value_pad[offset:offset + held_frames]).astype(jnp.float32)
        dot_list.append(jnp.einsum('ftnd,ftnd->ftn', grad_h, value_h))
    grad_dots = jnp.stack(dot_list)
    centre = lax.optimization_barrier(jnp.sum(soft_probs * grad_dots, axis=0, keepdims=True))
    score_grad = (soft_probs * (grad_dots - centre) * score_scale).astype(jnp.bfloat16)
    pad_shape = (key_pad.shape[0],) + query_h.shape[1:]
    query_grad = jnp.zeros(query_h.shape, jnp.float32)
    key_grad = jnp.zeros(pad_shape, jnp.float32)
    value_grad = jnp.zeros(pad_shape, jnp.float32)
    for offset in range(span_len):
        key_h = heads_of(key_pad[offset:offset + held_frames]).astype(jnp.float32)
        score_w = score_grad[offset][..., None].astype(jnp.float32)
        query_grad = query_grad + score_w * key_h
        key_grad = key_grad.at[offset:offset + held_frames].add(score_w * query_h)
        value_grad = value_grad.at[offset:offset + held_frames].add(weights_b[offset][..., None].astype(jnp.float32) * grad_h)
    flat_shape = (key_pad.shape[0],) + query_rows.shape[1:]
    pad_grad = jnp.concatenate([key_grad.reshape(flat_shape), value_grad.reshape(flat_shape)], -1)
    return (query_grad.reshape(query_rows.shape), pad_grad)

def reference(frames, norm_gain, w_qkv, w_out, cotangent):
    feat_width = D
    normed, unit_rows, spread = normalize(frames, norm_gain)
    qkv_rows = project(normed, w_qkv).astype(jnp.bfloat16)
    kv_pad = jnp.pad(qkv_rows[..., feat_width:], ((WINDOW, WINDOW), (0, 0), (0, 0)))
    query_rows = qkv_rows[..., :feat_width]
    mixed_rows, soft_probs, weights_b = attend(query_rows, kv_pad[..., :feat_width], kv_pad[..., feat_width:], 0, FRAMES, CLIP)
    block_out = (frames.astype(jnp.float32) + project(mixed_rows, w_out)).astype(jnp.bfloat16)
    out_grad = contract(mixed_rows, cotangent)
    grad_mix = project_back(cotangent, w_out).astype(jnp.bfloat16)
    query_grad, pad_grad = attend_back(query_rows, kv_pad[..., :feat_width], kv_pad[..., feat_width:], soft_probs, weights_b, grad_mix)
    kv_grad = pad_grad[WINDOW:WINDOW + FRAMES]
    qkv_rows_grad = jnp.concatenate([query_grad, kv_grad], -1).astype(jnp.bfloat16)
    qkv_grad = contract(normed, qkv_rows_grad)
    normed_grad = project_back(qkv_rows_grad, w_qkv)
    gain_part = lax.optimization_barrier(jnp.sum(normed_grad * unit_rows, axis=(0, 1)))
    frames_grad = (cotangent.astype(jnp.float32) + norm_back(normed_grad, unit_rows, spread, norm_gain)).astype(jnp.bfloat16)
    inv_root = 1.0 / math.sqrt(TOKENS)
    return (block_out, frames_grad, qkv_grad * inv_root, out_grad * inv_root, gain_part * inv_root)
```

```python
import functools
import math

import jax
import jax.numpy as jnp
from jax import lax
from jax.experimental import pallas as pl
from jax.experimental.pallas import tpu as pltpu
from jax.sharding import PartitionSpec as P

HEADS = 12
HEAD_DIM = 64
WINDOW = 4
CLIP_MAX = 256
EPSILON = 1e-06

BF = jnp.bfloat16
F32 = jnp.float32
AXES = ("tm", "inner")
VMEM_LIMIT = 60 * 1024 * 1024


def mm(a, b):
    return lax.dot_general(a, b, (((1,), (0,)), ((), ())), preferred_element_type=F32)


def mm_t(a, b):
    return lax.dot_general(a, b, (((1,), (1,)), ((), ())), preferred_element_type=F32)


def params():
    return pltpu.CompilerParams(vmem_limit_bytes=VMEM_LIMIT)


def row_stats(x):
    center = x - jnp.mean(x, axis=-1, keepdims=True)
    spread = lax.rsqrt(jnp.mean(center * center, axis=-1, keepdims=True) + EPSILON)
    return center * spread, spread


def forward_kernel(x_ref, gain_ref, wqkv_ref, wout_ref, bias_ref, nt_ref, q_ref, kt_ref, v_ref, prob_ref, mixt_ref, block_ref, n_ref, qkv_ref):
    tokens, width = x_ref.shape
    x = x_ref[...].astype(F32)
    unit, _ = row_stats(x)
    normed = unit * gain_ref[...]
    n_ref[...] = normed.astype(BF)
    nt_ref[...] = normed.T.astype(BF)
    step = 256

    def project(i, carry):
        cols = pl.ds(pl.multiple_of(i * step, step), step)
        qkv_ref[:, cols] = mm(n_ref[...], wqkv_ref[:, cols]).astype(BF)
        return carry

    lax.fori_loop(0, 3 * width // step, project, 0)
    q_ref[...] = qkv_ref[:, :width]
    v_ref[...] = qkv_ref[:, 2 * width :]
    scale = HEAD_DIM ** (-0.5)

    def pair(i, carry):
        cols = pl.ds(pl.multiple_of(i * 128, 128), 128)
        q2 = qkv_ref[:, cols]
        k2 = qkv_ref[:, pl.ds(pl.multiple_of(width + i * 128, 128), 128)]
        v2 = qkv_ref[:, pl.ds(pl.multiple_of(2 * width + i * 128, 128), 128)]
        kt_ref[cols, :] = k2.astype(F32).T.astype(BF)
        v2t = v2.astype(F32).T.astype(BF)
        for half in range(2):
            span = slice(half * 64, half * 64 + 64)
            scores = mm_t(k2[:, span], q2[:, span]) * scale + bias_ref[...]
            grown = jnp.exp(scores - jnp.max(scores, axis=0, keepdims=True))
            probs = grown / jnp.sum(grown, axis=0, keepdims=True)
            prob_ref[2 * i + half] = probs
            mixt = mm(v2t[span, :], probs.astype(BF))
            mixt_ref[pl.ds(pl.multiple_of(i * 128 + half * 64, 64), 64), :] = mixt.astype(BF)
        return carry

    lax.fori_loop(0, HEADS // 2, pair, 0)
    mixed = mixt_ref[...].astype(F32).T.astype(BF)
    block_ref[...] = (x + mm(mixed, wout_ref[...])).astype(BF)


def put_blocks(dst_ref, src):
    parts, _, wide = dst_ref.shape
    for j in range(parts):
        dst_ref[j] = src[:, j * wide : (j + 1) * wide]


def backward_kernel(cot_ref, wout_ref, q_ref, kt_ref, v_ref, prob_ref, dqkv_ref, dblk_ref, cblk_ref, gm_ref, dqt_ref):
    tokens, width = cot_ref.shape
    gm_ref[...] = mm_t(cot_ref[...], wout_ref[...]).astype(BF)
    put_blocks(cblk_ref, cot_ref[...])
    scale = HEAD_DIM ** (-0.5)

    def pair(i, carry):
        cols = pl.ds(pl.multiple_of(i * 128, 128), 128)
        q2 = q_ref[:, cols]
        g2 = gm_ref[:, cols]
        v2 = v_ref[:, cols]
        dks, dvs = [], []
        for half in range(2):
            span = slice(half * 64, half * 64 + 64)
            probs = prob_ref[2 * i + half]
            dots = mm_t(v2[:, span], g2[:, span])
            centre = jnp.sum(probs * dots, axis=0, keepdims=True)
            sgrad = (probs * (dots - centre) * scale).astype(BF)
            rows = pl.ds(pl.multiple_of(i * 128 + half * 64, 64), 64)
            dqt_ref[rows, :] = mm(kt_ref[rows, :], sgrad)
            dks.append(mm(sgrad, q2[:, span]))
            dvs.append(mm(probs.astype(BF), g2[:, span]))
        dqkv_ref[:, pl.ds(pl.multiple_of(width + i * 128, 128), 128)] = jnp.concatenate(dks, 1).astype(BF)
        dqkv_ref[:, pl.ds(pl.multiple_of(2 * width + i * 128, 128), 128)] = jnp.concatenate(dvs, 1).astype(BF)
        return carry

    lax.fori_loop(0, HEADS // 2, pair, 0)
    dqkv_ref[:, :width] = dqt_ref[...].T.astype(BF)
    put_blocks(dblk_ref, dqkv_ref[...])


def norm_kernel(x_ref, cot_ref, gain_ref, dqkv_ref, wqkv_ref, fgrad_ref, gpart_ref):
    x = x_ref[...].astype(F32)
    unit, spread = row_stats(x)
    ngrad = mm_t(dqkv_ref[...], wqkv_ref[...])
    gpart_ref[...] = jnp.sum(ngrad * unit, axis=0, keepdims=True)
    scaled = ngrad * gain_ref[...]
    mean_one = jnp.mean(scaled, axis=-1, keepdims=True)
    second = jnp.mean(scaled * unit, axis=-1, keepdims=True)
    fgrad_ref[...] = (cot_ref[...].astype(F32) + spread * (scaled - mean_one - unit * second)).astype(BF)


def block_sum(table, got, o, nt_ref, mt_ref, db_ref, cb_ref):
    row, run = table[o, 0], table[o, 1]
    left = mm(nt_ref[row], db_ref[run])
    right = mm(mt_ref[row], cb_ref[run])
    half = left.shape[0] // 2
    folded = jnp.concatenate([left[:half], left[half:], right[:half], right[half:]], 1)
    for s, ref in enumerate(got):
        folded = folded + ref[table[o, 2 + s]].astype(F32)
    return folded


def send_kernel(table, nt_ref, mt_ref, db_ref, cb_ref, *rest):
    got, out_ref = rest[:-1], rest[-1]

    def one(o, carry):
        out_ref[o] = block_sum(table, got, o, nt_ref, mt_ref, db_ref, cb_ref).astype(BF)
        return carry

    lax.fori_loop(0, out_ref.shape[0], one, 0)


def last_kernel(inv_root, table, nt_ref, mt_ref, db_ref, cb_ref, *rest):
    got, (q_ref, o_ref) = rest[:-2], rest[-2:]
    total = block_sum(table, got, 0, nt_ref, mt_ref, db_ref, cb_ref) * inv_root
    half = q_ref.shape[0] // 2
    wide, thin = q_ref.shape[1], o_ref.shape[1]
    q_ref[:half] = total[:, :wide]
    q_ref[half:] = total[:, wide : 2 * wide]
    o_ref[:half] = total[:, 2 * wide : 2 * wide + thin]
    o_ref[half:] = total[:, 2 * wide + thin :]


def squeeze_bits(value, bits):
    for b in sorted(bits, reverse=True):
        value = (value >> (b + 1) << b) | (value & ((1 << b) - 1))
    return value


def spread_bits(value, bits):
    for b in sorted(bits):
        value = (value >> b << (b + 1)) | (value & ((1 << b) - 1))
    return value


def reduce_weights(nt, mixt, dblk, cblk, inv_root):
    runs, inner = lax.axis_size("tm"), lax.axis_size("inner")
    row_bits, run_bits = (inner // 2).bit_length() - 1, runs.bit_length() - 1
    me_t, me_i = lax.axis_index("tm"), lax.axis_index("inner")
    core = me_i & 1
    mine = (me_t << row_bits) | (me_i >> 1)
    run_order = [row_bits + b for b in range(run_bits)]
    tail = list(range(row_bits))
    order = [run_order + tail, run_order[1:] + run_order[:1] + tail]
    rows = nt.shape[0] // inner
    tokens = nt.shape[1]
    nt = nt.reshape(inner, rows, tokens)
    mixt = mixt.reshape(inner, rows, tokens)
    wide, thin = dblk.shape[2], cblk.shape[2]
    folded = (rows // 2, 2 * (wide + thin))
    stages = len(order[0])
    got = []

    def table_of(stage):
        entries = []
        for c in range(2):
            past = order[c][: max(stage, 0)]
            here = [] if stage < 0 or stage == stages else [order[c][stage]]
            ids = jnp.arange(1 << (len(order[c]) - len(past) - len(here)), dtype=jnp.int32)
            ids = spread_bits(ids, past + here)
            for b in past:
                ids = ids | (mine & (1 << b))
            for b in here:
                ids = ids | ((mine ^ (1 << b)) & (1 << b))
            row = (ids & ((1 << row_bits) - 1)) * 2 + (1 - c if stage < 0 else c)
            cols = [row, ids >> row_bits]
            if stage >= 0:
                for s in range(stage + 1):
                    cols.append(squeeze_bits(ids, order[c][:s]))
            entries.append(jnp.stack(cols, 1))
        return jnp.where(core == 0, entries[0], entries[1]).astype(jnp.int32)

    def call(kernel, table, out_shape):
        args = [nt, mixt, dblk, cblk, *got]
        return pl.pallas_call(
            kernel,
            out_shape=out_shape,
            in_specs=[pl.BlockSpec(memory_space=pltpu.SMEM)] + [pl.BlockSpec(memory_space=pltpu.VMEM)] * len(args),
            compiler_params=params(),
        )(table, *args)

    for stage in range(-1, stages):
        table = table_of(stage)
        out = call(send_kernel, table, jax.ShapeDtypeStruct((table.shape[0],) + folded, BF))
        perm = []
        for t in range(runs):
            for i in range(inner):
                if stage < 0:
                    t2, i2 = t, i ^ 1
                else:
                    b = order[i & 1][stage]
                    t2 = t ^ (1 << (b - row_bits)) if b >= row_bits else t
                    i2 = i ^ (2 << b) if b < row_bits else i
                perm.append((t * inner + i, t2 * inner + i2))
        got.append(lax.ppermute(out, AXES, perm))
    return call(
        functools.partial(last_kernel, inv_root),
        table_of(stages),
        (jax.ShapeDtypeStruct((rows, wide), F32), jax.ShapeDtypeStruct((rows, thin), F32)),
    )


def to_tubes(rows, count):
    held, patches, width = rows.shape
    parts = jnp.moveaxis(rows.reshape(held, count, patches // count, width), 1, 0)
    parts = lax.all_to_all(parts, AXES, split_axis=0, concat_axis=0, tiled=True)
    return parts.reshape(-1, width)


def to_frames(tubes, count, held, patches):
    width = tubes.shape[1]
    parts = tubes.reshape(count, held, patches // count, width)
    parts = lax.all_to_all(parts, AXES, split_axis=0, concat_axis=0, tiled=True)
    return jnp.moveaxis(parts, 0, 1).reshape(held, patches, width)


def window_bias(all_frames, patches, clip_len):
    tokens = all_frames * patches
    key = lax.broadcasted_iota(jnp.int32, (tokens, tokens), 0)
    query = lax.broadcasted_iota(jnp.int32, (tokens, tokens), 1)
    key_f, query_f = key // patches, query // patches
    inside = (key % patches == query % patches) & (abs(key_f - query_f) <= WINDOW)
    inside = inside & (key_f // clip_len == query_f // clip_len)
    return jnp.where(inside, 0.0, -1e30).astype(F32)


def shards(frames, norm_gain, w_qkv, w_out, cotangent):
    held, patches, width = frames.shape
    runs, inner = lax.axis_size("tm"), lax.axis_size("inner")
    count = runs * inner
    all_frames = held * count
    clip_len = min(CLIP_MAX, all_frames)
    inv_root = 1.0 / math.sqrt(all_frames * patches)
    tokens = all_frames * patches // count
    gain = norm_gain.reshape(1, width)
    bias = window_bias(all_frames, patches // count, clip_len)

    x = to_tubes(frames, count)
    cot = to_tubes(cotangent, count)
    sds = jax.ShapeDtypeStruct
    nt, q, kt, v, prob, mixt, block = pl.pallas_call(
        forward_kernel,
        out_shape=(
            sds((width, tokens), BF),
            sds((tokens, width), BF),
            sds((width, tokens), BF),
            sds((tokens, width), BF),
            sds((HEADS, tokens, tokens), F32),
            sds((width, tokens), BF),
            sds((tokens, width), BF),
        ),
        scratch_shapes=[pltpu.VMEM((tokens, width), BF), pltpu.VMEM((tokens, 3 * width), BF)],
        compiler_params=params(),
    )(x, gain, w_qkv, w_out, bias)
    block_out = to_frames(block, count, held, patches)
    dqkv, dblk, cblk = pl.pallas_call(
        backward_kernel,
        out_shape=(
            sds((tokens, 3 * width), BF),
            sds((runs, tokens, 3 * width // runs), BF),
            sds((runs, tokens, width // runs), BF),
        ),
        scratch_shapes=[pltpu.VMEM((tokens, width), BF), pltpu.VMEM((width, tokens), F32)],
        compiler_params=params(),
    )(cot, w_out, q, kt, v, prob)
    fgrad, gpart = pl.pallas_call(
        norm_kernel,
        out_shape=(sds((tokens, width), BF), sds((1, width), F32)),
        compiler_params=params(),
    )(x, cot, gain, dqkv, w_qkv)
    frames_grad = to_frames(fgrad, count, held, patches)
    shares = jnp.broadcast_to(gpart.reshape(1, inner, width // inner), (runs, inner, width // inner))
    shares = lax.all_to_all(shares.reshape(count, 1, -1), AXES, split_axis=0, concat_axis=0, tiled=True)
    gain_grad = jnp.sum(shares, axis=(0, 1)) * inv_root
    qkv_grad, out_grad = reduce_weights(nt, mixt, dblk, cblk, inv_root)
    return block_out, frames_grad, qkv_grad, out_grad, gain_grad


def solution(mesh):
    in_specs = (P(AXES, None, None), P(), P(), P(), P(AXES, None, None))
    out_specs = (P(AXES, None, None), P(AXES, None, None), P("inner", "tm"), P("inner", "tm"), P("inner"))
    return jax.shard_map(shards, mesh=mesh, in_specs=in_specs, out_specs=out_specs, check_vma=False)
```

```python
import functools
import math

import jax
import jax.numpy as jnp
from jax import lax
from jax.experimental import pallas as pl
from jax.experimental.pallas import tpu as pltpu
from jax.sharding import PartitionSpec as P

HEADS = 12
HEAD_DIM = 64
WINDOW = 4
CLIP_MAX = 256
EPSILON = 1e-06
SCALE = HEAD_DIM ** (-0.5)

BF = jnp.bfloat16
F32 = jnp.float32
AXES = ("tm", "inner")
LANES = 128
VMEM_LIMIT = 60 * 1024 * 1024


def mm(a, b):
    return lax.dot_general(a, b, (((1,), (0,)), ((), ())), preferred_element_type=F32)


def mm_t(a, b):
    return lax.dot_general(a, b, (((1,), (1,)), ((), ())), preferred_element_type=F32)


def call(kernel, out_shape, *args, scratch=(), flops=0):
    leaves = jax.tree.leaves(out_shape) + list(args)
    moved = sum(math.prod(a.shape) * a.dtype.itemsize for a in leaves)
    return pl.pallas_call(
        kernel,
        out_shape=out_shape,
        scratch_shapes=scratch,
        compiler_params=pltpu.CompilerParams(vmem_limit_bytes=VMEM_LIMIT),
        cost_estimate=pl.CostEstimate(flops=flops, bytes_accessed=moved, transcendentals=0),
    )(*args)


def row_stats(x):
    center = x - jnp.mean(x, axis=-1, keepdims=True)
    spread = lax.rsqrt(jnp.mean(center * center, axis=-1, keepdims=True) + EPSILON)
    return center * spread, spread


def key_spans(tokens, reach):
    spans = []
    for start in range(0, tokens, LANES):
        low = max(0, start - reach) // 16 * 16
        high = min(tokens, -(-(start + LANES + reach) // 16) * 16)
        spans.append((start, low, high))
    return spans


def split_rows(mine_ref, other_ref, slot, src_ref, core):
    count, rows = mine_ref.shape[1], mine_ref.shape[2]
    for z in range(count):
        mine = src_ref[pl.ds(pl.multiple_of((2 * z + core) * rows, 8), rows), :]
        other = src_ref[pl.ds(pl.multiple_of((2 * z + 1 - core) * rows, 8), rows), :]
        mine_ref[slot, z] = mine.astype(BF)
        other_ref[slot, z] = other.astype(BF)


def forward_kernel(reach, x_ref, gain_ref, wqkv_ref, bias_ref, mine_ref, other_ref, q_ref, kt_ref, v_ref, prob_ref, mixed_ref, n_ref, k_ref, t_ref):
    tokens, width = x_ref.shape
    core = lax.axis_index("inner") & 1
    unit, _ = row_stats(x_ref[...].astype(F32))
    normed = unit * gain_ref[...]
    n_ref[...] = normed.astype(BF)
    t_ref[...] = normed.T
    split_rows(mine_ref, other_ref, 0, t_ref, core)
    step = 256

    def project(i, carry):
        cols = pl.ds(pl.multiple_of(i * step, step), step)
        k_cols = pl.ds(pl.multiple_of(width + i * step, step), step)
        v_cols = pl.ds(pl.multiple_of(2 * width + i * step, step), step)
        q_ref[:, cols] = (mm(n_ref[...], wqkv_ref[:, cols]) * SCALE).astype(BF)
        k_ref[:, cols] = mm(n_ref[...], wqkv_ref[:, k_cols]).astype(BF)
        v_ref[:, cols] = mm(n_ref[...], wqkv_ref[:, v_cols]).astype(BF)
        return carry

    lax.fori_loop(0, width // step, project, 0)

    def pair(i, carry):
        cols = pl.ds(pl.multiple_of(i * 128, 128), 128)
        q2, k2, v2 = q_ref[:, cols], k_ref[:, cols], v_ref[:, cols]
        kt_ref[cols, :] = (k2.astype(F32).T * SCALE).astype(BF)
        v2t = v2.astype(F32).T.astype(BF)
        for half in range(2):
            span = slice(half * 64, half * 64 + 64)
            for b, (start, low, high) in enumerate(key_spans(tokens, reach)):
                block = slice(start, start + LANES)
                scores = mm_t(k2[low:high, span], q2[block, span]) + bias_ref[low:high, block]
                grown = jnp.exp(scores - jnp.max(scores, axis=0, keepdims=True))
                probs = grown * (1.0 / jnp.sum(grown, axis=0, keepdims=True))
                prob_ref[2 * i + half, b, : high - low] = probs
                rows = pl.ds(pl.multiple_of(i * 128 + half * 64, 64), 64)
                mixt = mm(v2t[span, low:high], probs.astype(BF))
                t_ref[rows, block] = mixt
        return carry

    lax.fori_loop(0, HEADS // 2, pair, 0)
    mixed_ref[...] = t_ref[...].T.astype(BF)
    split_rows(mine_ref, other_ref, 1, t_ref, core)


def out_kernel(frames_ref, mixed_ref, wout_ref, out_ref):
    out_ref[...] = (frames_ref[...].astype(F32) + mm(mixed_ref[...], wout_ref[...])).astype(BF)


def put_blocks(dst_ref, src):
    parts, _, wide = dst_ref.shape
    for j in range(parts):
        dst_ref[j] = src[:, j * wide : (j + 1) * wide]


def blocks_kernel(cot_ref, other_ref, out_ref, out_other_ref):
    put_blocks(out_ref, cot_ref[...])
    put_blocks(out_other_ref, other_ref[...])


def backward_kernel(reach, cot_ref, wout_ref, q_ref, kt_ref, v_ref, prob_ref, dqkv_ref, dblk_ref, gm_ref, dqt_ref):
    tokens, width = cot_ref.shape
    gm_ref[...] = mm_t(cot_ref[...], wout_ref[...]).astype(BF)
    spans = key_spans(tokens, reach)

    def widen(parts):
        cols = []
        for part, (_, low, high) in zip(parts, spans):
            rows = [jnp.zeros((low, LANES), BF)] if low else []
            rows += [part]
            rows += [jnp.zeros((tokens - high, LANES), BF)] if high < tokens else []
            cols.append(jnp.concatenate(rows, 0) if len(rows) > 1 else part)
        return jnp.concatenate(cols, 1) if len(cols) > 1 else cols[0]

    def pair(i, carry):
        cols = pl.ds(pl.multiple_of(i * 128, 128), 128)
        q2, g2, v2, kt2 = q_ref[:, cols], gm_ref[:, cols], v_ref[:, cols], kt_ref[cols, :]
        dks, dvs = [], []
        for half in range(2):
            span = slice(half * 64, half * 64 + 64)
            weights, grads = [], []
            for b, (start, low, high) in enumerate(spans):
                block = slice(start, start + LANES)
                probs = prob_ref[2 * i + half, b, : high - low]
                dots = mm_t(v2[low:high, span], g2[block, span])
                centre = jnp.sum(probs * dots, axis=0, keepdims=True)
                sgrad = (probs * (dots - centre)).astype(BF)
                rows = pl.ds(pl.multiple_of(i * 128 + half * 64, 64), 64)
                dqt_ref[rows, block] = mm(kt2[span, low:high], sgrad)
                weights.append(probs.astype(BF))
                grads.append(sgrad)
            dks.append(mm(widen(grads), q2[:, span]))
            dvs.append(mm(widen(weights), g2[:, span]))
        dqkv_ref[:, pl.ds(pl.multiple_of(width + i * 128, 128), 128)] = jnp.concatenate(dks, 1).astype(BF)
        dqkv_ref[:, pl.ds(pl.multiple_of(2 * width + i * 128, 128), 128)] = jnp.concatenate(dvs, 1).astype(BF)
        return carry

    lax.fori_loop(0, HEADS // 2, pair, 0)
    dqkv_ref[:, :width] = dqt_ref[...].T.astype(BF)
    put_blocks(dblk_ref, dqkv_ref[...])


def norm_kernel(x_ref, cot_ref, gain_ref, dqkv_ref, wqkv_ref, fgrad_ref, gpart_ref):
    unit, spread = row_stats(x_ref[...].astype(F32))
    ngrad = mm_t(dqkv_ref[...], wqkv_ref[...])
    gpart_ref[...] = jnp.sum(ngrad * unit, axis=0, keepdims=True)
    scaled = ngrad * gain_ref[...]
    mean_one = jnp.mean(scaled, axis=-1, keepdims=True)
    second = jnp.mean(scaled * unit, axis=-1, keepdims=True)
    fgrad_ref[...] = (cot_ref[...].astype(F32) + spread * (scaled - mean_one - unit * second)).astype(BF)


def squeeze_bits(value, bits):
    for b in sorted(bits, reverse=True):
        value = (value >> (b + 1) << b) | (value & ((1 << b) - 1))
    return value


def spread_bits(value, bits):
    for b in sorted(bits):
        value = (value >> b << (b + 1)) | (value & ((1 << b) - 1))
    return value


def bit_orders(runs):
    bits = list(range(runs.bit_length() - 1))
    return bits, bits[1:] + bits[:1]


def place_of(runs, stage, n, send):
    me = lax.axis_index("tm")
    found = []
    for order in bit_orders(runs):
        past, bit = order[:stage], order[stage]
        run = spread_bits(n, past + [bit])
        for b in past:
            run = run | (me & (1 << b))
        run = run | ((me ^ (1 << bit) if send else me) & (1 << bit))
        found.append((run, squeeze_bits(run, past)))
    first = lax.axis_index("inner") & 1 == 0
    return jnp.where(first, found[0][0], found[1][0]), jnp.where(first, found[0][1], found[1][1])


def exchange(value, runs, inner, stage):
    perm = []
    for t in range(runs):
        for i in range(inner):
            t2 = t ^ (1 << bit_orders(runs)[i & 1][stage])
            perm.append((t * inner + i, t2 * inner + i))
    return lax.ppermute(value, AXES, perm)


def to_partner(value, inner):
    return lax.ppermute(value, "inner", [(i, i ^ 1) for i in range(inner)])


def product_kernel(runs, slot, send, mine_ref, other_ref, d_ref, d_other_ref, out_ref):
    count, rows, tokens = mine_ref.shape[1:]
    half = rows // 2
    left = mine_ref[slot].reshape(count * rows, tokens)
    right = other_ref[slot].reshape(count * rows, tokens)
    for n in range(out_ref.shape[0]):
        run, _ = place_of(runs, 0, n, send)
        total = mm(left, d_ref[run]) + mm(right, d_other_ref[run])
        for z in range(count):
            block = total[z * rows : (z + 1) * rows]
            out_ref[n, z] = jnp.concatenate([block[:half], block[half:]], 1).astype(out_ref.dtype)


def stage_kernel(runs, stage, send, keep_ref, got_ref, out_ref):
    for n in range(out_ref.shape[0]):
        _, place = place_of(runs, stage, n, send)
        out_ref[n] = (keep_ref[place] + got_ref[place].astype(F32)).astype(out_ref.dtype)


def start_reduce(slot, mine, other, d, d_other, runs):
    count, rows, tokens = mine.shape[1:]
    folded = (runs // 2, count, rows // 2, 2 * d.shape[2])
    flops = 2 * count * rows * 2 * tokens * d.shape[2] * (runs // 2)
    send = call(functools.partial(product_kernel, runs, slot, True), jax.ShapeDtypeStruct(folded, BF), mine, other, d, d_other, flops=flops)
    keep = call(functools.partial(product_kernel, runs, slot, False), jax.ShapeDtypeStruct(folded, F32), mine, other, d, d_other, flops=flops)
    return send, keep


def reduce_runs(send, keep, runs, inner):
    got = exchange(send, runs, inner, 0)
    for stage in range(1, runs.bit_length() - 1):
        shape = (keep.shape[0] // 2,) + keep.shape[1:]
        send = call(functools.partial(stage_kernel, runs, stage, True), jax.ShapeDtypeStruct(shape, BF), keep, got)
        keep = call(functools.partial(stage_kernel, runs, stage, False), jax.ShapeDtypeStruct(shape, F32), keep, got)
        got = exchange(send, runs, inner, stage)
    return keep, got


def rows_kernel(keep_ref, got_ref, keep_o_ref, got_o_ref, own_ref, *send_refs):
    count = keep_ref.shape[1]
    me = lax.axis_index("inner") >> 1

    def total(z):
        left = keep_ref[0, z] + got_ref[0, z].astype(F32)
        right = keep_o_ref[0, z] + got_o_ref[0, z].astype(F32)
        return jnp.concatenate([left, right], 1)

    for k, ref in enumerate(send_refs):
        ref[...] = total(lax.rem(me + k + 1, count)).astype(BF)
    own_ref[...] = total(me)


def last_kernel(inv_root, own_ref, *rest):
    got, (q_ref, o_ref) = rest[:-2], rest[-2:]
    total = own_ref[...]
    for ref in got:
        total = total + ref[...].astype(F32)
    total = total * inv_root
    half = q_ref.shape[0] // 2
    wide, thin = q_ref.shape[1], o_ref.shape[1]
    q_ref[:half] = total[:, :wide]
    q_ref[half:] = total[:, wide : 2 * wide]
    o_ref[:half] = total[:, 2 * wide : 2 * wide + thin]
    o_ref[half:] = total[:, 2 * wide + thin :]


def reduce_rows(parts_q, parts_o, inner, inv_root):
    _, count, half, wide = parts_q[0].shape
    thin = parts_o[0].shape[3]
    block = (half, wide + thin)
    sds = jax.ShapeDtypeStruct
    own, *sends = call(rows_kernel, (sds(block, F32),) + (sds(block, BF),) * (count - 1), *parts_q, *parts_o)
    got = []
    for k, send in enumerate(sends):
        got.append(lax.ppermute(send, "inner", [(i, (i + 2 * (k + 1)) % inner) for i in range(inner)]))
    out = (sds((2 * half, wide // 2), F32), sds((2 * half, thin // 2), F32))
    return call(functools.partial(last_kernel, inv_root), out, own, *got)


def to_tubes(rows, count):
    held, patches, width = rows.shape
    parts = jnp.moveaxis(rows.reshape(held, count, patches // count, width), 1, 0)
    parts = lax.all_to_all(parts, AXES, split_axis=0, concat_axis=0, tiled=True)
    return parts.reshape(-1, width)


def to_frames(tubes, count, held, patches):
    width = tubes.shape[1]
    parts = tubes.reshape(count, held, patches // count, width)
    parts = lax.all_to_all(parts, AXES, split_axis=0, concat_axis=0, tiled=True)
    return jnp.moveaxis(parts, 0, 1).reshape(held, patches, width)


def window_bias(all_frames, patches, clip_len):
    tokens = all_frames * patches
    key = lax.broadcasted_iota(jnp.int32, (tokens, tokens), 0)
    query = lax.broadcasted_iota(jnp.int32, (tokens, tokens), 1)
    key_f, query_f = key // patches, query // patches
    inside = (key % patches == query % patches) & (abs(key_f - query_f) <= WINDOW)
    inside = inside & (key_f // clip_len == query_f // clip_len)
    return jnp.where(inside, 0.0, -1e30).astype(F32)


def shards(frames, norm_gain, w_qkv, w_out, cotangent):
    held, patches, width = frames.shape
    runs, inner = lax.axis_size("tm"), lax.axis_size("inner")
    count = runs * inner
    all_frames = held * count
    clip_len = min(CLIP_MAX, all_frames)
    inv_root = 1.0 / math.sqrt(all_frames * patches)
    tokens = all_frames * patches // count
    reach = WINDOW * (patches // count)
    gain = norm_gain.reshape(1, width)
    bias = window_bias(all_frames, patches // count, clip_len)
    spans = key_spans(tokens, reach)
    longest = max(high - low for _, low, high in spans)
    sds = jax.ShapeDtypeStruct
    vmem = pltpu.VMEM

    x = to_tubes(frames, count)
    cot = to_tubes(cotangent, count)
    halves = sds((2, inner // 2, width // inner, tokens), BF)
    mine, other, q, kt, v, prob, mixed = call(
        functools.partial(forward_kernel, reach),
        (
            halves,
            halves,
            sds((tokens, width), BF),
            sds((width, tokens), BF),
            sds((tokens, width), BF),
            sds((HEADS, len(spans), longest, LANES), F32),
            sds((tokens, width), BF),
        ),
        x,
        gain,
        w_qkv,
        bias,
        scratch=[vmem((tokens, width), BF), vmem((tokens, width), BF), vmem((width, tokens), F32)],
        flops=2 * tokens * width * 4 * width,
    )
    theirs = to_partner(other, inner)
    mixed_back = to_frames(mixed, count, held, patches)
    block_out = call(out_kernel, sds((held * patches, width), BF), frames.reshape(-1, width), mixed_back.reshape(-1, width), w_out, flops=2 * tokens * width * width)
    block_out = block_out.reshape(held, patches, width)

    cblk = sds((runs, tokens, width // runs), BF)
    cblk, cblk_other = call(blocks_kernel, (cblk, cblk), cot, to_partner(cot, inner))
    parts_o = reduce_runs(*start_reduce(1, mine, theirs, cblk, cblk_other, runs), runs, inner)

    dqkv, dblk = call(
        functools.partial(backward_kernel, reach),
        (sds((tokens, 3 * width), BF), sds((runs, tokens, 3 * width // runs), BF)),
        cot,
        w_out,
        q,
        kt,
        v,
        prob,
        scratch=[vmem((tokens, width), BF), vmem((width, tokens), F32)],
        flops=2 * tokens * width * 4 * width,
    )
    dblk_other = to_partner(dblk, inner)
    fgrad, gpart = call(
        norm_kernel,
        (sds((tokens, width), BF), sds((1, width), F32)),
        x,
        cot,
        gain,
        dqkv,
        w_qkv,
        flops=2 * tokens * width * 3 * width,
    )
    frames_grad = to_frames(fgrad, count, held, patches)
    parts_q = reduce_runs(*start_reduce(0, mine, theirs, dblk, dblk_other, runs), runs, inner)
    qkv_grad, out_grad = reduce_rows(parts_q, parts_o, inner, inv_root)
    shares = jnp.broadcast_to(gpart.reshape(1, inner, width // inner), (runs, inner, width // inner))
    shares = lax.all_to_all(shares.reshape(count, 1, -1), AXES, split_axis=0, concat_axis=0, tiled=True)
    gain_grad = jnp.sum(shares, axis=(0, 1)) * inv_root
    return block_out, frames_grad, qkv_grad, out_grad, gain_grad


def solution(mesh):
    in_specs = (P(AXES, None, None), P(), P(), P(), P(AXES, None, None))
    out_specs = (P(AXES, None, None), P(AXES, None, None), P("inner", "tm"), P("inner", "tm"), P("inner"))
    return jax.shard_map(shards, mesh=mesh, in_specs=in_specs, out_specs=out_specs, check_vma=False)
```

```python
import functools
import math

import jax
import jax.numpy as jnp
from jax import lax
from jax.experimental import pallas as pl
from jax.experimental.pallas import tpu as pltpu
from jax.sharding import PartitionSpec as P


HEADS = 12
HEAD_DIM = 64
WINDOW = 4
CLIP_MAX = 256
EPSILON = 1e-06
SCALE = HEAD_DIM ** (-0.5)

BF = jnp.bfloat16
F32 = jnp.float32
AXES = ("tm", "inner")
LANES = 128
VMEM_SPARE = 8 * 1024 * 1024


def mm(a, b):
    return lax.dot_general(a, b, (((1,), (0,)), ((), ())), preferred_element_type=F32)


def mm_t(a, b):
    return lax.dot_general(a, b, (((1,), (1,)), ((), ())), preferred_element_type=F32)


def call(kernel, out_shape, *args, scratch=(), flops=0):
    def size(arrays):
        return sum(math.prod(a.shape) * jnp.dtype(a.dtype).itemsize for a in arrays)

    moved = size(jax.tree.leaves(out_shape) + list(args))
    return pl.pallas_call(
        kernel,
        out_shape=out_shape,
        scratch_shapes=scratch,
        compiler_params=pltpu.CompilerParams(vmem_limit_bytes=moved + size(scratch) + VMEM_SPARE),
        cost_estimate=pl.CostEstimate(flops=flops, bytes_accessed=moved, transcendentals=0),
    )(*args)


def row_stats(x):
    center = x - jnp.mean(x, axis=-1, keepdims=True)
    spread = lax.rsqrt(jnp.mean(center * center, axis=-1, keepdims=True) + EPSILON)
    return center * spread, spread


def key_spans(tokens, reach):
    spans = []
    for start in range(0, tokens, LANES):
        low = max(0, start - reach) // 16 * 16
        high = min(tokens, -(-(start + LANES + reach) // 16) * 16)
        spans.append((start, low, high))
    return spans


def split_rows(mine_ref, other_ref, slot, src_ref, core):
    count, rows = mine_ref.shape[1], mine_ref.shape[2]
    for z in range(count):
        mine = src_ref[pl.ds(pl.multiple_of((2 * z + core) * rows, 8), rows), :]
        other = src_ref[pl.ds(pl.multiple_of((2 * z + 1 - core) * rows, 8), rows), :]
        mine_ref[slot, z] = mine.astype(BF)
        other_ref[slot, z] = other.astype(BF)


def forward_kernel(reach, x_ref, gain_ref, wqkv_ref, bias_ref, mine_ref, other_ref, q_ref, kt_ref, v_ref, prob_ref, mixed_ref, n_ref, k_ref, t_ref):
    tokens, width = x_ref.shape
    core = lax.axis_index("inner") & 1
    unit, _ = row_stats(x_ref[...].astype(F32))
    normed = unit * gain_ref[...]
    n_ref[...] = normed.astype(BF)
    t_ref[...] = normed.T
    split_rows(mine_ref, other_ref, 0, t_ref, core)
    step = 256

    def project(i, carry):
        cols = pl.ds(pl.multiple_of(i * step, step), step)
        k_cols = pl.ds(pl.multiple_of(width + i * step, step), step)
        v_cols = pl.ds(pl.multiple_of(2 * width + i * step, step), step)
        q_ref[:, cols] = (mm(n_ref[...], wqkv_ref[:, cols]) * SCALE).astype(BF)
        k_ref[:, cols] = mm(n_ref[...], wqkv_ref[:, k_cols]).astype(BF)
        v_ref[:, cols] = mm(n_ref[...], wqkv_ref[:, v_cols]).astype(BF)
        return carry

    lax.fori_loop(0, width // step, project, 0)

    def pair(i, carry):
        cols = pl.ds(pl.multiple_of(i * 128, 128), 128)
        q2, k2, v2 = q_ref[:, cols], k_ref[:, cols], v_ref[:, cols]
        kt_ref[cols, :] = (k2.astype(F32).T * SCALE).astype(BF)
        v2t = v2.astype(F32).T.astype(BF)
        for half in range(2):
            span = slice(half * 64, half * 64 + 64)
            for b, (start, low, high) in enumerate(key_spans(tokens, reach)):
                block = slice(start, start + LANES)
                scores = mm_t(k2[low:high, span], q2[block, span]) + bias_ref[low:high, block]
                grown = jnp.exp(scores - jnp.max(scores, axis=0, keepdims=True))
                probs = grown * (1.0 / jnp.sum(grown, axis=0, keepdims=True))
                prob_ref[2 * i + half, b, : high - low] = probs
                rows = pl.ds(pl.multiple_of(i * 128 + half * 64, 64), 64)
                mixt = mm(v2t[span, low:high], probs.astype(BF))
                t_ref[rows, block] = mixt
        return carry

    lax.fori_loop(0, HEADS // 2, pair, 0)
    mixed_ref[...] = t_ref[...].T.astype(BF)
    split_rows(mine_ref, other_ref, 1, t_ref, core)


def out_kernel(frames_ref, mixed_ref, wout_ref, out_ref):
    out_ref[...] = (frames_ref[...].astype(F32) + mm(mixed_ref[...], wout_ref[...])).astype(BF)


def backward_kernel(reach, cot_ref, wout_ref, q_ref, kt_ref, v_ref, prob_ref, dqkv_ref, gm_ref, dqt_ref):
    tokens, width = cot_ref.shape
    gm_ref[...] = mm_t(cot_ref[...], wout_ref[...]).astype(BF)
    spans = key_spans(tokens, reach)

    def widen(parts):
        cols = []
        for part, (_, low, high) in zip(parts, spans):
            rows = [jnp.zeros((low, LANES), BF)] if low else []
            rows += [part]
            rows += [jnp.zeros((tokens - high, LANES), BF)] if high < tokens else []
            cols.append(jnp.concatenate(rows, 0) if len(rows) > 1 else part)
        return jnp.concatenate(cols, 1) if len(cols) > 1 else cols[0]

    def pair(i, carry):
        cols = pl.ds(pl.multiple_of(i * 128, 128), 128)
        q2, g2, v2, kt2 = q_ref[:, cols], gm_ref[:, cols], v_ref[:, cols], kt_ref[cols, :]
        dks, dvs = [], []
        for half in range(2):
            span = slice(half * 64, half * 64 + 64)
            weights, grads = [], []
            for b, (start, low, high) in enumerate(spans):
                block = slice(start, start + LANES)
                probs = prob_ref[2 * i + half, b, : high - low]
                dots = mm_t(v2[low:high, span], g2[block, span])
                centre = jnp.sum(probs * dots, axis=0, keepdims=True)
                sgrad = (probs * (dots - centre)).astype(BF)
                rows = pl.ds(pl.multiple_of(i * 128 + half * 64, 64), 64)
                dqt_ref[rows, block] = mm(kt2[span, low:high], sgrad)
                weights.append(probs.astype(BF))
                grads.append(sgrad)
            dks.append(mm(widen(grads), q2[:, span]))
            dvs.append(mm(widen(weights), g2[:, span]))
        dqkv_ref[:, pl.ds(pl.multiple_of(width + i * 128, 128), 128)] = jnp.concatenate(dks, 1).astype(BF)
        dqkv_ref[:, pl.ds(pl.multiple_of(2 * width + i * 128, 128), 128)] = jnp.concatenate(dvs, 1).astype(BF)
        return carry

    lax.fori_loop(0, HEADS // 2, pair, 0)
    dqkv_ref[:, :width] = dqt_ref[...].T.astype(BF)


def norm_kernel(x_ref, cot_ref, gain_ref, dqkv_ref, wqkv_ref, fgrad_ref, gpart_ref):
    unit, spread = row_stats(x_ref[...].astype(F32))
    ngrad = mm_t(dqkv_ref[...], wqkv_ref[...])
    gpart_ref[...] = jnp.sum(ngrad * unit, axis=0, keepdims=True)
    scaled = ngrad * gain_ref[...]
    mean_one = jnp.mean(scaled, axis=-1, keepdims=True)
    second = jnp.mean(scaled * unit, axis=-1, keepdims=True)
    fgrad_ref[...] = (cot_ref[...].astype(F32) + spread * (scaled - mean_one - unit * second)).astype(BF)


def squeeze_bits(value, bits):
    for b in sorted(bits, reverse=True):
        value = (value >> (b + 1) << b) | (value & ((1 << b) - 1))
    return value


def spread_bits(value, bits):
    for b in sorted(bits):
        value = (value >> b << (b + 1)) | (value & ((1 << b) - 1))
    return value


def bit_orders(runs):
    bits = list(range(runs.bit_length() - 1))
    return bits, bits[1:] + bits[:1]


def place_of(runs, stage, n, send):
    me = lax.axis_index("tm")
    found = []
    for order in bit_orders(runs):
        past, bit = order[:stage], order[stage]
        run = spread_bits(n, past + [bit])
        for b in past:
            run = run | (me & (1 << b))
        run = run | ((me ^ (1 << bit) if send else me) & (1 << bit))
        found.append((run, squeeze_bits(run, past)))
    first = lax.axis_index("inner") & 1 == 0
    return jnp.where(first, found[0][0], found[1][0]), jnp.where(first, found[0][1], found[1][1])


def exchange(value, runs, inner, stage):
    perm = []
    for t in range(runs):
        for i in range(inner):
            t2 = t ^ (1 << bit_orders(runs)[i & 1][stage])
            perm.append((t * inner + i, t2 * inner + i))
    return lax.ppermute(value, AXES, perm)


def to_partner(value, inner):
    return lax.ppermute(value, "inner", [(i, i ^ 1) for i in range(inner)])


def product_kernel(runs, send, mine_ref, other_ref, d_ref, d_other_ref, c_ref, c_other_ref, out_ref, dblk_ref, cblk_ref):
    count, rows, tokens = mine_ref.shape[1:]
    half = rows // 2
    for p, (d, c) in enumerate(((d_ref, c_ref), (d_other_ref, c_other_ref))):
        for dst, src in ((dblk_ref, d), (cblk_ref, c)):
            wide = dst.shape[3]
            for j in range(runs):
                dst[p, j] = src[:, j * wide : (j + 1) * wide]
    for n in range(out_ref.shape[0]):
        run, _ = place_of(runs, 0, n, send)
        first = 0
        for slot, blocks in ((0, dblk_ref), (1, cblk_ref)):
            left = mine_ref[slot].reshape(count * rows, tokens)
            right = other_ref[slot].reshape(count * rows, tokens)
            total = mm(left, blocks[0, run]) + mm(right, blocks[1, run])
            wide = 2 * total.shape[1]
            for z in range(count):
                block = total[z * rows : (z + 1) * rows]
                out_ref[n, z, :, first : first + wide] = jnp.concatenate([block[:half], block[half:]], 1).astype(out_ref.dtype)
            first += wide


def stage_kernel(runs, stage, send, keep_ref, got_ref, out_ref):
    for n in range(out_ref.shape[0]):
        _, place = place_of(runs, stage, n, send)
        out_ref[n] = (keep_ref[place] + got_ref[place].astype(F32)).astype(out_ref.dtype)


def reduce_runs(mine, other, d, d_other, c, c_other, runs, inner):
    count, rows, tokens = mine.shape[1:]
    wide, thin = d.shape[1] // runs, c.shape[1] // runs
    shape = (runs // 2, count, rows // 2, 2 * (wide + thin))
    flops = 2 * count * rows * 2 * tokens * (wide + thin) * (runs // 2)
    scratch = [pltpu.VMEM((2, runs, tokens, wide), BF), pltpu.VMEM((2, runs, tokens, thin), BF)]
    args = (mine, other, d, d_other, c, c_other)
    send = call(functools.partial(product_kernel, runs, True), jax.ShapeDtypeStruct(shape, BF), *args, scratch=scratch, flops=flops)
    got = exchange(send, runs, inner, 0)
    keep = call(functools.partial(product_kernel, runs, False), jax.ShapeDtypeStruct(shape, F32), *args, scratch=scratch, flops=flops)
    for stage in range(1, runs.bit_length() - 1):
        shape = (shape[0] // 2,) + shape[1:]
        send = call(functools.partial(stage_kernel, runs, stage, True), jax.ShapeDtypeStruct(shape, BF), keep, got)
        later = exchange(send, runs, inner, stage)
        keep = call(functools.partial(stage_kernel, runs, stage, False), jax.ShapeDtypeStruct(shape, F32), keep, got)
        got = later
    return keep, got


def rows_kernel(keep_ref, got_ref, own_ref, *send_refs):
    count = keep_ref.shape[1]
    me = lax.axis_index("inner") >> 1

    def total(z):
        return keep_ref[0, z] + got_ref[0, z].astype(F32)

    for k, ref in enumerate(send_refs):
        ref[...] = total(lax.rem(me + k + 1, count)).astype(BF)
    own_ref[...] = total(me)


def last_kernel(inv_root, own_ref, *rest):
    got, (q_ref, o_ref) = rest[:-2], rest[-2:]
    total = own_ref[...]
    for ref in got:
        total = total + ref[...].astype(F32)
    total = total * inv_root
    half = q_ref.shape[0] // 2
    wide, thin = q_ref.shape[1], o_ref.shape[1]
    q_ref[:half] = total[:, :wide]
    q_ref[half:] = total[:, wide : 2 * wide]
    o_ref[:half] = total[:, 2 * wide : 2 * wide + thin]
    o_ref[half:] = total[:, 2 * wide + thin :]


def reduce_rows(keep, got, wide, thin, inner, inv_root):
    _, count, half, lanes = keep.shape
    block = (half, lanes)
    sds = jax.ShapeDtypeStruct
    own, *sends = call(rows_kernel, (sds(block, F32),) + (sds(block, BF),) * (count - 1), keep, got)
    got = []
    for k, send in enumerate(sends):
        got.append(lax.ppermute(send, "inner", [(i, (i + 2 * (k + 1)) % inner) for i in range(inner)]))
    out = (sds((2 * half, wide), F32), sds((2 * half, thin), F32))
    return call(functools.partial(last_kernel, inv_root), out, own, *got)


def to_tubes(rows, count):
    held, patches, width = rows.shape
    parts = jnp.moveaxis(rows.reshape(held, count, patches // count, width), 1, 0)
    parts = lax.all_to_all(parts, AXES, split_axis=0, concat_axis=0, tiled=True)
    return parts.reshape(-1, width)


def to_frames(tubes, count, held, patches):
    width = tubes.shape[1]
    parts = tubes.reshape(count, held, patches // count, width)
    parts = lax.all_to_all(parts, AXES, split_axis=0, concat_axis=0, tiled=True)
    return jnp.moveaxis(parts, 0, 1).reshape(held, patches, width)


def window_bias(all_frames, patches, clip_len):
    tokens = all_frames * patches
    key = lax.broadcasted_iota(jnp.int32, (tokens, tokens), 0)
    query = lax.broadcasted_iota(jnp.int32, (tokens, tokens), 1)
    key_f, query_f = key // patches, query // patches
    inside = (key % patches == query % patches) & (abs(key_f - query_f) <= WINDOW)
    inside = inside & (key_f // clip_len == query_f // clip_len)
    return jnp.where(inside, 0.0, -1e30).astype(F32)


def shards(frames, norm_gain, w_qkv, w_out, cotangent):
    held, patches, width = frames.shape
    runs, inner = lax.axis_size("tm"), lax.axis_size("inner")
    count = runs * inner
    all_frames = held * count
    clip_len = min(CLIP_MAX, all_frames)
    inv_root = 1.0 / math.sqrt(all_frames * patches)
    tokens = all_frames * patches // count
    reach = WINDOW * (patches // count)
    gain = norm_gain.reshape(1, width)
    bias = window_bias(all_frames, patches // count, clip_len)
    spans = key_spans(tokens, reach)
    longest = max(high - low for _, low, high in spans)
    sds = jax.ShapeDtypeStruct
    vmem = pltpu.VMEM

    x = to_tubes(frames, count)
    cot = to_tubes(cotangent, count)
    halves = sds((2, inner // 2, width // inner, tokens), BF)
    mine, other, q, kt, v, prob, mixed = call(
        functools.partial(forward_kernel, reach),
        (
            halves,
            halves,
            sds((tokens, width), BF),
            sds((width, tokens), BF),
            sds((tokens, width), BF),
            sds((HEADS, len(spans), longest, LANES), F32),
            sds((tokens, width), BF),
        ),
        x,
        gain,
        w_qkv,
        bias,
        scratch=[vmem((tokens, width), BF), vmem((tokens, width), BF), vmem((width, tokens), F32)],
        flops=2 * tokens * width * 4 * width,
    )
    theirs = to_partner(other, inner)
    mixed_back = to_frames(mixed, count, held, patches)
    block_out = call(out_kernel, sds((held * patches, width), BF), frames.reshape(-1, width), mixed_back.reshape(-1, width), w_out, flops=2 * tokens * width * width)
    block_out = block_out.reshape(held, patches, width)
    cot_other = to_partner(cot, inner)
    dqkv = call(
        functools.partial(backward_kernel, reach),
        sds((tokens, 3 * width), BF),
        cot,
        w_out,
        q,
        kt,
        v,
        prob,
        scratch=[vmem((tokens, width), BF), vmem((width, tokens), F32)],
        flops=2 * tokens * width * 4 * width,
    )
    dqkv_other = to_partner(dqkv, inner)
    fgrad, gpart = call(
        norm_kernel,
        (sds((tokens, width), BF), sds((1, width), F32)),
        x,
        cot,
        gain,
        dqkv,
        w_qkv,
        flops=2 * tokens * width * 3 * width,
    )
    frames_grad = to_frames(fgrad, count, held, patches)
    keep, got = reduce_runs(mine, theirs, dqkv, dqkv_other, cot, cot_other, runs, inner)
    qkv_grad, out_grad = reduce_rows(keep, got, 3 * width // runs, width // runs, inner, inv_root)
    shares = jnp.broadcast_to(gpart.reshape(1, inner, width // inner), (runs, inner, width // inner))
    shares = lax.all_to_all(shares.reshape(count, 1, -1), AXES, split_axis=0, concat_axis=0, tiled=True)
    gain_grad = jnp.sum(shares, axis=(0, 1)) * inv_root
    return block_out, frames_grad, qkv_grad, out_grad, gain_grad


def solution(mesh):
    in_specs = (P(AXES, None, None), P(), P(), P(), P(AXES, None, None))
    out_specs = (P(AXES, None, None), P(AXES, None, None), P("inner", "tm"), P("inner", "tm"), P("inner"))
    return jax.shard_map(shards, mesh=mesh, in_specs=in_specs, out_specs=out_specs, check_vma=False)
```

```python
import functools
import math

import jax
import jax.numpy as jnp
from jax import lax
from jax.experimental import pallas as pl
from jax.experimental.pallas import tpu as pltpu
from jax.sharding import PartitionSpec as P


HEADS = 12
HEAD_DIM = 64
WINDOW = 4
CLIP_MAX = 256
EPSILON = 1e-06
SCALE = HEAD_DIM ** (-0.5)

BF = jnp.bfloat16
F32 = jnp.float32
AXES = ("tm", "inner")
LANES = 128
VMEM_SPARE = 8 * 1024 * 1024
PIECES = 2


def mm(a, b):
    return lax.dot_general(a, b, (((1,), (0,)), ((), ())), preferred_element_type=F32)


def mm_t(a, b):
    return lax.dot_general(a, b, (((1,), (1,)), ((), ())), preferred_element_type=F32)


def call(kernel, out_shape, *args, scratch=(), flops=0, raw_in=(), raw_out=(), copies=0):
    outs = jax.tree.leaves(out_shape)

    def size(arrays):
        return sum(math.prod(a.shape) * jnp.dtype(a.dtype).itemsize for a in arrays)

    def spec(raw):
        return pl.BlockSpec(memory_space=pltpu.HBM if raw else pltpu.VMEM)

    moved = size(outs) + size(args)
    out_specs = [spec(i in raw_out) for i in range(len(outs))]
    taken = size(a for i, a in enumerate(args) if i not in raw_in) + size(a for i, a in enumerate(outs) if i not in raw_out)
    semaphores = [pltpu.SemaphoreType.DMA((copies,))] if copies else []
    placed = [pltpu.HBM(a.shape, a.dtype) for a in outs]
    args = [pltpu.with_memory_space_constraint(a, pltpu.HBM) if i in raw_in else a for i, a in enumerate(args)]
    return pl.pallas_call(
        kernel,
        out_shape=placed if isinstance(out_shape, (tuple, list)) else placed[0],
        in_specs=[spec(i in raw_in) for i in range(len(args))],
        out_specs=out_specs if isinstance(out_shape, (tuple, list)) else out_specs[0],
        scratch_shapes=list(scratch) + semaphores,
        compiler_params=pltpu.CompilerParams(vmem_limit_bytes=taken + size(scratch) + VMEM_SPARE),
        cost_estimate=pl.CostEstimate(flops=flops, bytes_accessed=moved, transcendentals=0),
    )(*args)


def row_stats(x):
    center = x - jnp.mean(x, axis=-1, keepdims=True)
    spread = lax.rsqrt(jnp.mean(center * center, axis=-1, keepdims=True) + EPSILON)
    return center * spread, spread


def key_spans(tokens, reach):
    spans = []
    for start in range(0, tokens, LANES):
        low = max(0, start - reach) // 16 * 16
        high = min(tokens, -(-(start + LANES + reach) // 16) * 16)
        spans.append((start, low, high))
    return spans


def split_rows(mine_ref, other_ref, slot, src_ref, core):
    pieces, count, rows = mine_ref.shape[1:4]
    for z in range(count):
        for dst, which in ((mine_ref, core), (other_ref, 1 - core)):
            start = pl.multiple_of((2 * z + which) * pieces * rows, 8)
            block = src_ref[pl.ds(start, pieces * rows), :].astype(BF)
            for p in range(pieces):
                dst[slot, p, z] = block[p * rows : (p + 1) * rows]


def forward_kernel(reach, x_ref, gain_ref, bias_ref, wqkv_hbm, *rest):
    outs, (wqkv_ref, mine_ref, other_ref, q_ref, kt_ref, v_ref, prob_ref, mixed_ref, n_ref, k_ref, t_ref, sem) = rest[:7], rest[7:]
    tokens, width = x_ref.shape
    core = lax.axis_index("inner") & 1
    loads = []
    for part in range(3):
        cols = pl.ds(part * width, width)
        loads.append(pltpu.make_async_copy(wqkv_hbm.at[:, cols], wqkv_ref.at[part], sem.at[part]))
        loads[-1].start()
    sources = (mine_ref, other_ref, q_ref, kt_ref, v_ref, prob_ref, mixed_ref)
    stores = {i: pltpu.make_async_copy(sources[i], outs[i], sem.at[3 + i]) for i in (0, 1, 2, 3, 4, 6)}
    unit, _ = row_stats(x_ref[...].astype(F32))
    normed = unit * gain_ref[...]
    n_ref[...] = normed.astype(BF)
    t_ref[...] = normed.T
    split_rows(mine_ref, other_ref, 0, t_ref, core)
    step = 256
    for part, (dst, factor) in enumerate(((q_ref, SCALE), (k_ref, 1.0), (v_ref, 1.0))):
        loads[part].wait()
        for i in range(width // step):
            cols = slice(i * step, (i + 1) * step)
            dst[:, cols] = (mm(n_ref[...], wqkv_ref[part, :, cols]) * factor).astype(BF)
        if part != 1:
            stores[2 + part].start()

    def prob_store(i):
        heads = pl.ds(2 * i, 2)
        return pltpu.make_async_copy(prob_ref.at[heads], outs[5].at[heads], sem.at[10 + i])

    def pair(i, carry):
        cols = pl.ds(pl.multiple_of(i * 128, 128), 128)
        q2, k2, v2 = q_ref[:, cols], k_ref[:, cols], v_ref[:, cols]
        kt_ref[cols, :] = (k2.astype(F32).T * SCALE).astype(BF)
        v2t = v2.astype(F32).T.astype(BF)
        for half in range(2):
            span = slice(half * 64, half * 64 + 64)
            for b, (start, low, high) in enumerate(key_spans(tokens, reach)):
                block = slice(start, start + LANES)
                scores = mm_t(k2[low:high, span], q2[block, span]) + bias_ref[low:high, block]
                grown = jnp.exp(scores - jnp.max(scores, axis=0, keepdims=True))
                probs = grown * (1.0 / jnp.sum(grown, axis=0, keepdims=True))
                prob_ref[2 * i + half, b, : high - low] = probs
                rows = pl.ds(pl.multiple_of(i * 128 + half * 64, 64), 64)
                mixt = mm(v2t[span, low:high], probs.astype(BF))
                t_ref[rows, block] = mixt
        prob_store(i).start()
        return carry

    lax.fori_loop(0, HEADS // 2, pair, 0)
    stores[3].start()
    mixed_ref[...] = t_ref[...].T.astype(BF)
    stores[6].start()
    split_rows(mine_ref, other_ref, 1, t_ref, core)
    stores[0].start()
    stores[1].start()

    def finish(i, carry):
        prob_store(i).wait()
        return carry

    lax.fori_loop(0, HEADS // 2, finish, 0)
    for store in stores.values():
        store.wait()


def out_kernel(frames_ref, mixed_ref, wout_ref, out_ref):
    out_ref[...] = (frames_ref[...].astype(F32) + mm(mixed_ref[...], wout_ref[...])).astype(BF)


def copy_kernel(src_ref, dst_ref):
    dst_ref[...] = src_ref[...]


def backward_kernel(reach, cot_ref, *rest):
    sources, (dqkv_hbm, blocks_hbm), rest = rest[:5], rest[5:7], rest[7:]
    wout_ref, q_ref, kt_ref, v_ref, prob_ref, dqkv_ref, blocks_ref, gm_ref, dqt_ref, sem = rest
    tokens, width = cot_ref.shape
    targets = (wout_ref, q_ref, kt_ref, v_ref, prob_ref)
    loads = [pltpu.make_async_copy(src, dst, sem.at[i]) for i, (src, dst) in enumerate(zip(sources, targets))]
    for load in loads:
        load.start()
    loads[0].wait()
    gm_ref[...] = mm_t(cot_ref[...], wout_ref[...]).astype(BF)
    for load in loads[1:]:
        load.wait()
    spans = key_spans(tokens, reach)

    def widen(parts):
        cols = []
        for part, (_, low, high) in zip(parts, spans):
            rows = [jnp.zeros((low, LANES), BF)] if low else []
            rows += [part]
            rows += [jnp.zeros((tokens - high, LANES), BF)] if high < tokens else []
            cols.append(jnp.concatenate(rows, 0) if len(rows) > 1 else part)
        return jnp.concatenate(cols, 1) if len(cols) > 1 else cols[0]

    def pair(i, carry):
        cols = pl.ds(pl.multiple_of(i * 128, 128), 128)
        q2, g2, v2, kt2 = q_ref[:, cols], gm_ref[:, cols], v_ref[:, cols], kt_ref[cols, :]
        dks, dvs = [], []
        for half in range(2):
            span = slice(half * 64, half * 64 + 64)
            weights, grads = [], []
            for b, (start, low, high) in enumerate(spans):
                block = slice(start, start + LANES)
                probs = prob_ref[2 * i + half, b, : high - low]
                dots = mm_t(v2[low:high, span], g2[block, span])
                centre = jnp.sum(probs * dots, axis=0, keepdims=True)
                sgrad = (probs * (dots - centre)).astype(BF)
                rows = pl.ds(pl.multiple_of(i * 128 + half * 64, 64), 64)
                dqt_ref[rows, block] = mm(kt2[span, low:high], sgrad)
                weights.append(probs.astype(BF))
                grads.append(sgrad)
            dks.append(mm(widen(grads), q2[:, span]))
            dvs.append(mm(widen(weights), g2[:, span]))
        dqkv_ref[:, pl.ds(pl.multiple_of(width + i * 128, 128), 128)] = jnp.concatenate(dks, 1).astype(BF)
        dqkv_ref[:, pl.ds(pl.multiple_of(2 * width + i * 128, 128), 128)] = jnp.concatenate(dvs, 1).astype(BF)
        return carry

    lax.fori_loop(0, HEADS // 2, pair, 0)
    dqkv_ref[:, :width] = dqt_ref[...].T.astype(BF)
    whole = pltpu.make_async_copy(dqkv_ref, dqkv_hbm, sem.at[5])
    runs = blocks_ref.shape[0]
    wide, thin = 3 * width // runs, width // runs
    stores = []
    for j in range(runs):
        blocks_ref[j, :, :wide] = dqkv_ref[:, j * wide : (j + 1) * wide]
        blocks_ref[j, :, wide:] = cot_ref[:, j * thin : (j + 1) * thin]
        stores.append(pltpu.make_async_copy(blocks_ref.at[j], blocks_hbm.at[j], sem.at[6 + j]))
        stores[-1].start()
    whole.start()
    for store in stores + [whole]:
        store.wait()


def norm_kernel(x_ref, cot_ref, gain_ref, dqkv_ref, wqkv_ref, fgrad_ref, gpart_ref):
    unit, spread = row_stats(x_ref[...].astype(F32))
    ngrad = mm_t(dqkv_ref[...], wqkv_ref[...])
    gpart_ref[...] = jnp.sum(ngrad * unit, axis=0, keepdims=True)
    scaled = ngrad * gain_ref[...]
    mean_one = jnp.mean(scaled, axis=-1, keepdims=True)
    second = jnp.mean(scaled * unit, axis=-1, keepdims=True)
    fgrad_ref[...] = (cot_ref[...].astype(F32) + spread * (scaled - mean_one - unit * second)).astype(BF)


def squeeze_bits(value, bits):
    for b in sorted(bits, reverse=True):
        value = (value >> (b + 1) << b) | (value & ((1 << b) - 1))
    return value


def spread_bits(value, bits):
    for b in sorted(bits):
        value = (value >> b << (b + 1)) | (value & ((1 << b) - 1))
    return value


def bit_orders(runs):
    bits = list(range(runs.bit_length() - 1))
    return bits, bits[1:] + bits[:1]


def by_core(values):
    return jnp.where(lax.axis_index("inner") & 1 == 0, *values)


def run_of(runs, stage, n, send):
    me = lax.axis_index("tm")
    found = []
    for order in bit_orders(runs):
        past, bit = order[:stage], order[stage]
        run = spread_bits(n, past + [bit])
        for b in past:
            run = run | (me & (1 << b))
        found.append(run | ((me ^ (1 << bit) if send else me) & (1 << bit)))
    return by_core(found)


def place_of(runs, stage, run):
    return by_core([squeeze_bits(run, order[: stage + 1]) for order in bit_orders(runs)])


def exchange(value, runs, inner, stage):
    perm = []
    for t in range(runs):
        for i in range(inner):
            t2 = t ^ (1 << bit_orders(runs)[i & 1][stage])
            perm.append((t * inner + i, t2 * inner + i))
    return lax.ppermute(value, AXES, perm)


def to_partner(value, inner):
    return lax.ppermute(value, "inner", [(i, i ^ 1) for i in range(inner)])


def product_kernel(runs, pieces, send, mine_ref, other_ref, d_ref, d_other_ref, *out_refs):
    _, _, count, rows, tokens = mine_ref.shape
    for piece, out_ref in zip(pieces, out_refs):
        wide = out_ref.shape[3] * 3 // 4
        for n in range(out_ref.shape[0]):
            run = run_of(runs, 0, n, send)
            totals = []
            for slot, cols in ((0, slice(0, wide)), (1, slice(wide, None))):
                left = mine_ref[slot, piece].reshape(count * rows, tokens)
                right = other_ref[slot, piece].reshape(count * rows, tokens)
                totals.append(mm(left, d_ref[run][:, cols]) + mm(right, d_other_ref[run][:, cols]))
            total = jnp.concatenate(totals, 1).astype(out_ref.dtype)
            for z in range(count):
                out_ref[n, z] = total[z * rows : (z + 1) * rows]


def partial_sum(runs, run, keep_ref, got_refs, z):
    total = keep_ref[place_of(runs, 0, run), z]
    for stage, ref in enumerate(got_refs):
        total = total + ref[place_of(runs, stage, run), z].astype(F32)
    return total


def stage_kernel(runs, stage, keep_ref, *rest):
    got_refs, out_ref = rest[:-1], rest[-1]
    for n in range(out_ref.shape[0]):
        run = run_of(runs, stage, n, True)
        for z in range(out_ref.shape[1]):
            out_ref[n, z] = partial_sum(runs, run, keep_ref, got_refs, z).astype(BF)


def rows_kernel(runs, keep_ref, *rest):
    stages = runs.bit_length() - 1
    got_refs, own_ref, send_refs = rest[:stages], rest[stages], rest[stages + 1 :]
    count = keep_ref.shape[1]
    me, run = lax.axis_index("inner") >> 1, lax.axis_index("tm")
    for k, ref in enumerate(send_refs):
        ref[...] = partial_sum(runs, run, keep_ref, got_refs, lax.rem(me + k + 1, count)).astype(BF)
    own_ref[...] = partial_sum(runs, run, keep_ref, got_refs, me)


def last_kernel(inv_root, pieces, *rest):
    got, (q_ref, o_ref) = rest[:-2], rest[-2:]
    rows, wide = q_ref.shape[0] // pieces, q_ref.shape[1]
    each = len(got) // pieces
    for p in range(pieces):
        own_ref, *others = got[p * each : (p + 1) * each]
        total = own_ref[...]
        for ref in others:
            total = total + ref[...].astype(F32)
        total = total * inv_root
        q_ref[p * rows : (p + 1) * rows] = total[:, :wide]
        o_ref[p * rows : (p + 1) * rows] = total[:, wide:]


def reduce_weights(mine, other, d, d_other, runs, inner, inv_root):
    sds = jax.ShapeDtypeStruct
    _, pieces, count, rows, tokens = mine.shape
    lanes = d.shape[2]
    stages = runs.bit_length() - 1
    shape = (runs // 2, count, rows, lanes)
    flops = 4 * count * rows * tokens * lanes * (runs // 2)
    args = (mine, other, d, d_other)
    got = [[] for _ in range(pieces)]
    for p in range(pieces):
        send = call(functools.partial(product_kernel, runs, (p,), True), (sds(shape, BF),), *args, flops=flops)[0]
        got[p].append(exchange(send, runs, inner, 0))
    keep = call(functools.partial(product_kernel, runs, tuple(range(pieces)), False), (sds(shape, F32),) * pieces, *args, flops=pieces * flops)
    for stage in range(1, stages):
        shape = (shape[0] // 2,) + shape[1:]
        for p in range(pieces):
            send = call(functools.partial(stage_kernel, runs, stage), sds(shape, BF), keep[p], *got[p])
            got[p].append(exchange(send, runs, inner, stage))
    last = []
    block = (rows, lanes)
    for p in range(pieces):
        own, *sends = call(functools.partial(rows_kernel, runs), (sds(block, F32),) + (sds(block, BF),) * (count - 1), keep[p], *got[p])
        last.append(own)
        for k, send in enumerate(sends):
            last.append(lax.ppermute(send, "inner", [(i, (i + 2 * (k + 1)) % inner) for i in range(inner)]))
    out = (sds((pieces * rows, lanes * 3 // 4), F32), sds((pieces * rows, lanes // 4), F32))
    return call(functools.partial(last_kernel, inv_root, pieces), out, *last)


def to_tubes(rows, count):
    held, patches, width = rows.shape
    parts = jnp.moveaxis(rows.reshape(held, count, patches // count, width), 1, 0)
    parts = lax.all_to_all(parts, AXES, split_axis=0, concat_axis=0, tiled=True)
    return parts.reshape(-1, width)


def to_frames(tubes, count, held, patches):
    width = tubes.shape[1]
    parts = tubes.reshape(count, held, patches // count, width)
    parts = lax.all_to_all(parts, AXES, split_axis=0, concat_axis=0, tiled=True)
    return jnp.moveaxis(parts, 0, 1).reshape(held, patches, width)


def window_bias(all_frames, patches, clip_len):
    tokens = all_frames * patches
    key = lax.broadcasted_iota(jnp.int32, (tokens, tokens), 0)
    query = lax.broadcasted_iota(jnp.int32, (tokens, tokens), 1)
    key_f, query_f = key // patches, query // patches
    inside = (key % patches == query % patches) & (abs(key_f - query_f) <= WINDOW)
    inside = inside & (key_f // clip_len == query_f // clip_len)
    return jnp.where(inside, 0.0, -1e30).astype(F32)


def shards(frames, norm_gain, w_qkv, w_out, cotangent):
    held, patches, width = frames.shape
    runs, inner = lax.axis_size("tm"), lax.axis_size("inner")
    count = runs * inner
    all_frames = held * count
    clip_len = min(CLIP_MAX, all_frames)
    inv_root = 1.0 / math.sqrt(all_frames * patches)
    tokens = all_frames * patches // count
    reach = WINDOW * (patches // count)
    gain = norm_gain.reshape(1, width)
    bias = window_bias(all_frames, patches // count, clip_len)
    spans = key_spans(tokens, reach)
    longest = max(high - low for _, low, high in spans)
    sds = jax.ShapeDtypeStruct
    vmem = pltpu.VMEM

    x = to_tubes(frames, count)
    cot = to_tubes(cotangent, count)
    halves = ((2, PIECES, inner // 2, width // inner // PIECES, tokens), BF)
    flat, turned = ((tokens, width), BF), ((width, tokens), BF)
    probs = ((HEADS, len(spans), longest, LANES), F32)
    made = (halves, halves, flat, turned, flat, probs, flat)
    mine, other, q, kt, v, prob, mixed = call(
        functools.partial(forward_kernel, reach),
        tuple(sds(*each) for each in made),
        x,
        gain,
        bias,
        w_qkv,
        scratch=[vmem((3, width, width), BF), *(vmem(*each) for each in made), vmem(*flat), vmem(*flat), vmem((width, tokens), F32)],
        flops=2 * tokens * width * 4 * width,
        raw_in=(3,),
        raw_out=range(7),
        copies=10 + HEADS // 2,
    )
    theirs = to_partner(other, inner)
    mixed_back = to_frames(mixed, count, held, patches)
    block_out = call(out_kernel, sds((held * patches, width), BF), frames.reshape(-1, width), mixed_back.reshape(-1, width), w_out, flops=2 * tokens * width * width)
    block_out = block_out.reshape(held, patches, width)
    made = (((tokens, 3 * width), BF), ((runs, tokens, 4 * width // runs), BF))
    dqkv, blocks = call(
        functools.partial(backward_kernel, reach),
        tuple(sds(*each) for each in made),
        cot,
        w_out,
        q,
        kt,
        v,
        prob,
        scratch=[*(vmem(*each) for each in (((width, width), BF), flat, turned, flat, probs) + made), vmem(*flat), vmem((width, tokens), F32)],
        flops=2 * tokens * width * 4 * width,
        raw_in=range(1, 6),
        raw_out=range(2),
        copies=6 + runs,
    )
    blocks_other = to_partner(blocks, inner)
    fgrad, gpart = call(
        norm_kernel,
        (sds((tokens, width), BF), sds((1, width), F32)),
        x,
        cot,
        gain,
        dqkv,
        w_qkv,
        flops=2 * tokens * width * 3 * width,
    )
    frames_grad = to_frames(fgrad, count, held, patches)
    frames_grad = call(copy_kernel, sds((held * patches, width), BF), frames_grad.reshape(-1, width)).reshape(held, patches, width)
    qkv_grad, out_grad = reduce_weights(mine, theirs, blocks, blocks_other, runs, inner, inv_root)
    shares = jnp.broadcast_to(gpart.reshape(1, inner, width // inner), (runs, inner, width // inner))
    shares = lax.all_to_all(shares.reshape(count, 1, -1), AXES, split_axis=0, concat_axis=0, tiled=True)
    gain_grad = jnp.sum(shares, axis=(0, 1)) * inv_root
    return block_out, frames_grad, qkv_grad, out_grad, gain_grad


def solution(mesh):
    in_specs = (P(AXES, None, None), P(), P(), P(), P(AXES, None, None))
    out_specs = (P(AXES, None, None), P(AXES, None, None), P("inner", "tm"), P("inner", "tm"), P("inner"))
    return jax.shard_map(shards, mesh=mesh, in_specs=in_specs, out_specs=out_specs, check_vma=False)
```

```python
import functools
import math

import jax
import jax.numpy as jnp
from jax import lax
from jax.experimental import pallas as pl
from jax.experimental.pallas import tpu as pltpu
from jax.sharding import PartitionSpec as P


HEADS = 12
HEAD_DIM = 64
WINDOW = 4
CLIP_MAX = 256
EPSILON = 1e-06
SCALE = HEAD_DIM ** (-0.5)

BF = jnp.bfloat16
F32 = jnp.float32
AXES = ("tm", "inner")
LANES = 128
VMEM_SPARE = 8 * 1024 * 1024
PIECES = 2
FRONT_UNROLL = 1
BACK_UNROLL = 2


def mm(a, b):
    return lax.dot_general(a, b, (((1,), (0,)), ((), ())), preferred_element_type=F32)


def mm_t(a, b):
    return lax.dot_general(a, b, (((1,), (1,)), ((), ())), preferred_element_type=F32)


def call(kernel, out_shape, *args, scratch=(), flops=0, raw_in=(), raw_out=(), copies=0):
    outs = jax.tree.leaves(out_shape)

    def size(arrays):
        return sum(math.prod(a.shape) * jnp.dtype(a.dtype).itemsize for a in arrays)

    def spec(raw):
        return pl.BlockSpec(memory_space=pltpu.HBM if raw else pltpu.VMEM)

    moved = size(outs) + size(args)
    out_specs = [spec(i in raw_out) for i in range(len(outs))]
    taken = size(a for i, a in enumerate(args) if i not in raw_in) + size(a for i, a in enumerate(outs) if i not in raw_out)
    semaphores = [pltpu.SemaphoreType.DMA((copies,))] if copies else []
    placed = [pltpu.HBM(a.shape, a.dtype) if i in raw_out else a for i, a in enumerate(outs)]
    args = [pltpu.with_memory_space_constraint(a, pltpu.HBM) if i in raw_in else a for i, a in enumerate(args)]
    return pl.pallas_call(
        kernel,
        out_shape=placed if isinstance(out_shape, (tuple, list)) else placed[0],
        in_specs=[spec(i in raw_in) for i in range(len(args))],
        out_specs=out_specs if isinstance(out_shape, (tuple, list)) else out_specs[0],
        scratch_shapes=list(scratch) + semaphores,
        compiler_params=pltpu.CompilerParams(vmem_limit_bytes=taken + size(scratch) + VMEM_SPARE),
        cost_estimate=pl.CostEstimate(flops=flops, bytes_accessed=moved, transcendentals=0),
    )(*args)


def row_stats(x):
    center = x - jnp.mean(x, axis=-1, keepdims=True)
    spread = lax.rsqrt(jnp.mean(center * center, axis=-1, keepdims=True) + EPSILON)
    return center * spread, spread


def key_spans(tokens, reach):
    spans = []
    for start in range(0, tokens, LANES):
        low = max(0, start - reach) // 16 * 16
        high = min(tokens, -(-(start + LANES + reach) // 16) * 16)
        spans.append((start, low, high))
    return spans


def split_rows(mine_ref, other_ref, slot, src_ref, core):
    pieces, count, rows = mine_ref.shape[1:4]
    for z in range(count):
        for dst, which in ((mine_ref, core), (other_ref, 1 - core)):
            start = pl.multiple_of((2 * z + which) * pieces * rows, 8)
            block = src_ref[pl.ds(start, pieces * rows), :].astype(BF)
            for p in range(pieces):
                dst[slot, p, z] = block[p * rows : (p + 1) * rows]


def forward_kernel(reach, x_ref, gain_ref, bias_ref, wqkv_hbm, *rest):
    outs, (wqkv_ref, mine_ref, other_ref, q_ref, kt_ref, v_ref, prob_ref, mixed_ref, n_ref, k_ref, t_ref, sem) = rest[:7], rest[7:]
    tokens, width = x_ref.shape
    core = lax.axis_index("inner") & 1
    loads = []
    for part in range(3):
        cols = pl.ds(part * width, width)
        loads.append(pltpu.make_async_copy(wqkv_hbm.at[:, cols], wqkv_ref.at[part], sem.at[part]))
        loads[-1].start()
    sources = (mine_ref, other_ref, q_ref, kt_ref, v_ref, prob_ref, mixed_ref)
    stores = {i: pltpu.make_async_copy(sources[i], outs[i], sem.at[3 + i]) for i in (0, 1, 2, 3, 4, 6)}
    unit, _ = row_stats(x_ref[...].astype(F32))
    normed = unit * gain_ref[...]
    n_ref[...] = normed.astype(BF)
    t_ref[...] = normed.T
    split_rows(mine_ref, other_ref, 0, t_ref, core)
    step = 256
    for part, (dst, factor) in enumerate(((q_ref, SCALE), (k_ref, 1.0), (v_ref, 1.0))):
        loads[part].wait()
        for i in range(width // step):
            cols = slice(i * step, (i + 1) * step)
            dst[:, cols] = (mm(n_ref[...], wqkv_ref[part, :, cols]) * factor).astype(BF)
        if part != 1:
            stores[2 + part].start()

    def prob_store(i):
        heads = pl.ds(2 * i, 2)
        return pltpu.make_async_copy(prob_ref.at[heads], outs[5].at[heads], sem.at[10 + i])

    def pair(i, carry):
        cols = pl.ds(pl.multiple_of(i * 128, 128), 128)
        q2, k2, v2 = q_ref[:, cols], k_ref[:, cols], v_ref[:, cols]
        kt_ref[cols, :] = (k2.astype(F32).T * SCALE).astype(BF)
        v2t = v2.astype(F32).T.astype(BF)
        for half in range(2):
            span = slice(half * 64, half * 64 + 64)
            for b, (start, low, high) in enumerate(key_spans(tokens, reach)):
                block = slice(start, start + LANES)
                scores = mm_t(k2[low:high, span], q2[block, span]) + bias_ref[low:high, block]
                grown = jnp.exp(scores - jnp.max(scores, axis=0, keepdims=True))
                probs = grown * (1.0 / jnp.sum(grown, axis=0, keepdims=True))
                prob_ref[2 * i + half, b, : high - low] = probs
                rows = pl.ds(pl.multiple_of(i * 128 + half * 64, 64), 64)
                mixt = mm(v2t[span, low:high], probs.astype(BF))
                t_ref[rows, block] = mixt
        prob_store(i).start()
        return carry

    lax.fori_loop(0, HEADS // 2, pair, 0, unroll=FRONT_UNROLL)
    stores[3].start()
    mixed_ref[...] = t_ref[...].T.astype(BF)
    stores[6].start()
    split_rows(mine_ref, other_ref, 1, t_ref, core)
    stores[0].start()
    stores[1].start()

    def finish(i, carry):
        prob_store(i).wait()
        return carry

    lax.fori_loop(0, HEADS // 2, finish, 0)
    for store in stores.values():
        store.wait()


def backward_kernel(reach, cot_ref, *rest):
    sources, blocks_ref, rest = rest[:5], rest[5], rest[6:]
    wout_ref, q_ref, kt_ref, v_ref, prob_ref, dqkv_ref, gm_ref, dqt_ref, sem = rest
    tokens, width = cot_ref.shape
    targets = (wout_ref, q_ref, kt_ref, v_ref, prob_ref)
    loads = [pltpu.make_async_copy(src, dst, sem.at[i]) for i, (src, dst) in enumerate(zip(sources, targets))]
    for load in loads:
        load.start()
    loads[0].wait()
    gm_ref[...] = mm_t(cot_ref[...], wout_ref[...]).astype(BF)
    for load in loads[1:]:
        load.wait()
    spans = key_spans(tokens, reach)

    def widen(parts):
        cols = []
        for part, (_, low, high) in zip(parts, spans):
            rows = [jnp.zeros((low, LANES), BF)] if low else []
            rows += [part]
            rows += [jnp.zeros((tokens - high, LANES), BF)] if high < tokens else []
            cols.append(jnp.concatenate(rows, 0) if len(rows) > 1 else part)
        return jnp.concatenate(cols, 1) if len(cols) > 1 else cols[0]

    def pair(i, carry):
        cols = pl.ds(pl.multiple_of(i * 128, 128), 128)
        q2, g2, v2, kt2 = q_ref[:, cols], gm_ref[:, cols], v_ref[:, cols], kt_ref[cols, :]
        dks, dvs = [], []
        for half in range(2):
            span = slice(half * 64, half * 64 + 64)
            weights, grads = [], []
            for b, (start, low, high) in enumerate(spans):
                block = slice(start, start + LANES)
                probs = prob_ref[2 * i + half, b, : high - low]
                dots = mm_t(v2[low:high, span], g2[block, span])
                centre = jnp.sum(probs * dots, axis=0, keepdims=True)
                sgrad = (probs * (dots - centre)).astype(BF)
                rows = pl.ds(pl.multiple_of(i * 128 + half * 64, 64), 64)
                dqt_ref[rows, block] = mm(kt2[span, low:high], sgrad)
                weights.append(probs.astype(BF))
                grads.append(sgrad)
            dks.append(mm(widen(grads), q2[:, span]))
            dvs.append(mm(widen(weights), g2[:, span]))
        dqkv_ref[:, pl.ds(pl.multiple_of(width + i * 128, 128), 128)] = jnp.concatenate(dks, 1).astype(BF)
        dqkv_ref[:, pl.ds(pl.multiple_of(2 * width + i * 128, 128), 128)] = jnp.concatenate(dvs, 1).astype(BF)
        return carry

    lax.fori_loop(0, HEADS // 2, pair, 0, unroll=BACK_UNROLL)
    dqkv_ref[:, :width] = dqt_ref[...].T.astype(BF)
    runs = blocks_ref.shape[0]
    wide, thin = 3 * width // runs, width // runs
    for j in range(runs):
        blocks_ref[j, :, :wide] = dqkv_ref[:, j * wide : (j + 1) * wide]
        blocks_ref[j, :, wide:] = cot_ref[:, j * thin : (j + 1) * thin]


def norm_kernel(inner, x_ref, cot_ref, gain_ref, blocks_ref, wqkv_ref, mixed_ref, back_ref, dqkv_ref, extra_ref):
    tokens, width = x_ref.shape
    runs = blocks_ref.shape[0]
    wide = 3 * width // runs
    for j in range(runs):
        dqkv_ref[:, j * wide : (j + 1) * wide] = blocks_ref[j, :, :wide]
    unit, spread = row_stats(x_ref[...].astype(F32))
    ngrad = mm_t(dqkv_ref[...], wqkv_ref[...])
    part = jnp.sum(ngrad * unit, axis=0, keepdims=True)
    scaled = ngrad * gain_ref[...]
    mean_one = jnp.mean(scaled, axis=-1, keepdims=True)
    second = jnp.mean(scaled * unit, axis=-1, keepdims=True)
    back_ref[:, :width] = mixed_ref[...]
    back_ref[:, width : 2 * width] = (cot_ref[...].astype(F32) + spread * (scaled - mean_one - unit * second)).astype(BF)
    high = part.astype(BF).astype(F32)
    extra_ref[...] = jnp.zeros_like(extra_ref)
    share, each = width // inner, tokens // (runs * inner)
    for k, value in enumerate((high, part - high)):
        row, lane = k % each, k // each * LANES
        for i in range(inner):
            piece = value[:, i * share : (i + 1) * share]
            for t in range(runs):
                start = (t * inner + i) * each + row
                extra_ref[start : start + 1, lane : lane + share] = piece
    back_ref[:, 2 * width :] = extra_ref[...].astype(BF)


def finish_kernel(inv_root, frames_ref, wout_ref, back_ref, block_ref, fgrad_ref, gain_ref):
    width, share = fgrad_ref.shape[1], gain_ref.shape[1]
    block_ref[...] = (frames_ref[...].astype(F32) + mm(back_ref[:, :width], wout_ref[...])).astype(BF)
    fgrad_ref[...] = back_ref[:, width : 2 * width]
    total = jnp.sum(back_ref[:, 2 * width :].astype(F32), axis=0, keepdims=True)
    parts = [total[:, k : k + share] for k in range(0, total.shape[1], LANES)]
    gain_ref[...] = sum(parts) * inv_root


def squeeze_bits(value, bits):
    for b in sorted(bits, reverse=True):
        value = (value >> (b + 1) << b) | (value & ((1 << b) - 1))
    return value


def spread_bits(value, bits):
    for b in sorted(bits):
        value = (value >> b << (b + 1)) | (value & ((1 << b) - 1))
    return value


def bit_orders(runs):
    bits = list(range(runs.bit_length() - 1))
    return bits, bits[1:] + bits[:1]


def by_core(values):
    return jnp.where(lax.axis_index("inner") & 1 == 0, *values)


def run_of(runs, stage, n, send):
    me = lax.axis_index("tm")
    found = []
    for order in bit_orders(runs):
        past, bit = order[:stage], order[stage]
        run = spread_bits(n, past + [bit])
        for b in past:
            run = run | (me & (1 << b))
        found.append(run | ((me ^ (1 << bit) if send else me) & (1 << bit)))
    return by_core(found)


def place_of(runs, stage, run):
    return by_core([squeeze_bits(run, order[: stage + 1]) for order in bit_orders(runs)])


def exchange(value, runs, inner, stage):
    perm = []
    for t in range(runs):
        for i in range(inner):
            t2 = t ^ (1 << bit_orders(runs)[i & 1][stage])
            perm.append((t * inner + i, t2 * inner + i))
    return lax.ppermute(value, AXES, perm)


def to_partner(value, inner):
    return lax.ppermute(value, "inner", [(i, i ^ 1) for i in range(inner)])


def product_kernel(runs, pieces, send, mine_ref, other_ref, d_ref, d_other_ref, *out_refs):
    _, _, count, rows, tokens = mine_ref.shape
    for piece, out_ref in zip(pieces, out_refs):
        wide = out_ref.shape[3] * 3 // 4
        for n in range(out_ref.shape[0]):
            run = run_of(runs, 0, n, send)
            totals = []
            for slot, cols in ((0, slice(0, wide)), (1, slice(wide, None))):
                left = mine_ref[slot, piece].reshape(count * rows, tokens)
                right = other_ref[slot, piece].reshape(count * rows, tokens)
                totals.append(mm(left, d_ref[run, :, cols]) + mm(right, d_other_ref[run, :, cols]))
            total = jnp.concatenate(totals, 1).astype(out_ref.dtype)
            for z in range(count):
                out_ref[n, z] = total[z * rows : (z + 1) * rows]


def partial_sum(runs, run, keep_ref, got_refs, z):
    total = keep_ref[place_of(runs, 0, run), z]
    for stage, ref in enumerate(got_refs):
        total = total + ref[place_of(runs, stage, run), z].astype(F32)
    return total


def stage_kernel(runs, stage, keep_ref, *rest):
    got_refs, out_ref = rest[:-1], rest[-1]
    for n in range(out_ref.shape[0]):
        run = run_of(runs, stage, n, True)
        for z in range(out_ref.shape[1]):
            out_ref[n, z] = partial_sum(runs, run, keep_ref, got_refs, z).astype(BF)


def rows_kernel(runs, keep_ref, *rest):
    stages = runs.bit_length() - 1
    got_refs, own_ref, send_refs = rest[:stages], rest[stages], rest[stages + 1 :]
    count = keep_ref.shape[1]
    me, run = lax.axis_index("inner") >> 1, lax.axis_index("tm")
    for k, ref in enumerate(send_refs):
        ref[...] = partial_sum(runs, run, keep_ref, got_refs, lax.rem(me + k + 1, count)).astype(BF)
    own_ref[...] = partial_sum(runs, run, keep_ref, got_refs, me)


def last_kernel(inv_root, pieces, *rest):
    got, (q_ref, o_ref) = rest[:-2], rest[-2:]
    rows, wide = q_ref.shape[0] // pieces, q_ref.shape[1]
    each = len(got) // pieces
    for p in range(pieces):
        own_ref, *others = got[p * each : (p + 1) * each]
        total = own_ref[...]
        for ref in others:
            total = total + ref[...].astype(F32)
        total = total * inv_root
        q_ref[p * rows : (p + 1) * rows] = total[:, :wide]
        o_ref[p * rows : (p + 1) * rows] = total[:, wide:]


def reduce_weights(mine, other, d, d_other, runs, inner, inv_root):
    sds = jax.ShapeDtypeStruct
    _, pieces, count, rows, tokens = mine.shape
    lanes = d.shape[2]
    stages = runs.bit_length() - 1
    shape = (runs // 2, count, rows, lanes)
    flops = 4 * count * rows * tokens * lanes * (runs // 2)
    args = (mine, other, d, d_other)

    def product(chosen, send, dtype):
        out = (sds(shape, dtype),) * len(chosen)
        return call(functools.partial(product_kernel, runs, chosen, send), out, *args, flops=len(chosen) * flops)

    got = [[] for _ in range(pieces)]
    for p in range(pieces):
        send = product((p,), True, BF)[0]
        got[p].append(exchange(send, runs, inner, 0))
    keep = product(tuple(range(pieces)), False, F32)
    for stage in range(1, stages):
        shape = (shape[0] // 2,) + shape[1:]
        for p in range(pieces):
            send = call(functools.partial(stage_kernel, runs, stage), sds(shape, BF), keep[p], *got[p])
            got[p].append(exchange(send, runs, inner, stage))
    last = []
    block = (rows, lanes)
    for p in range(pieces):
        own, *sends = call(functools.partial(rows_kernel, runs), (sds(block, F32),) + (sds(block, BF),) * (count - 1), keep[p], *got[p])
        last.append(own)
        for k, send in enumerate(sends):
            last.append(lax.ppermute(send, "inner", [(i, (i + 2 * (k + 1)) % inner) for i in range(inner)]))
    out = (sds((pieces * rows, lanes * 3 // 4), F32), sds((pieces * rows, lanes // 4), F32))
    return call(functools.partial(last_kernel, inv_root, pieces), out, *last)


def to_tubes(rows, count):
    held, patches, width = rows.shape
    parts = jnp.moveaxis(rows.reshape(held, count, patches // count, width), 1, 0)
    parts = lax.all_to_all(parts, AXES, split_axis=0, concat_axis=0, tiled=True)
    return parts.reshape(-1, width)


def to_frames(tubes, count, held, patches):
    width = tubes.shape[1]
    parts = tubes.reshape(count, held, patches // count, width)
    parts = lax.all_to_all(parts, AXES, split_axis=0, concat_axis=0, tiled=True)
    return jnp.moveaxis(parts, 0, 1).reshape(held, patches, width)


def window_bias(all_frames, patches, clip_len):
    tokens = all_frames * patches
    key = lax.broadcasted_iota(jnp.int32, (tokens, tokens), 0)
    query = lax.broadcasted_iota(jnp.int32, (tokens, tokens), 1)
    key_f, query_f = key // patches, query // patches
    inside = (key % patches == query % patches) & (abs(key_f - query_f) <= WINDOW)
    inside = inside & (key_f // clip_len == query_f // clip_len)
    return jnp.where(inside, 0.0, -1e30).astype(F32)


def shards(frames, norm_gain, w_qkv, w_out, cotangent):
    held, patches, width = frames.shape
    runs, inner = lax.axis_size("tm"), lax.axis_size("inner")
    count = runs * inner
    all_frames = held * count
    clip_len = min(CLIP_MAX, all_frames)
    inv_root = 1.0 / math.sqrt(all_frames * patches)
    tokens = all_frames * patches // count
    reach = WINDOW * (patches // count)
    gain = norm_gain.reshape(1, width)
    bias = window_bias(all_frames, patches // count, clip_len)
    spans = key_spans(tokens, reach)
    longest = max(high - low for _, low, high in spans)
    sds = jax.ShapeDtypeStruct
    vmem = pltpu.VMEM

    x = to_tubes(frames, count)
    cot = to_tubes(cotangent, count)
    halves = ((2, PIECES, inner // 2, width // inner // PIECES, tokens), BF)
    flat, turned = ((tokens, width), BF), ((width, tokens), BF)
    probs = ((HEADS, len(spans), longest, LANES), F32)
    made = (halves, halves, flat, turned, flat, probs, flat)
    mine, other, q, kt, v, prob, mixed = call(
        functools.partial(forward_kernel, reach),
        tuple(sds(*each) for each in made),
        x,
        gain,
        bias,
        w_qkv,
        scratch=[vmem((3, width, width), BF), *(vmem(*each) for each in made), vmem(*flat), vmem(*flat), vmem((width, tokens), F32)],
        flops=2 * tokens * width * 4 * width,
        raw_in=(3,),
        raw_out=range(7),
        copies=10 + HEADS // 2,
    )
    theirs = to_partner(other, inner)
    made = ((runs, tokens, 4 * width // runs), BF)
    blocks = call(
        functools.partial(backward_kernel, reach),
        sds(*made),
        cot,
        w_out,
        q,
        kt,
        v,
        prob,
        scratch=[*(vmem(*each) for each in (((width, width), BF), flat, turned, flat, probs)), vmem((tokens, 3 * width), BF), vmem(*flat), vmem((width, tokens), F32)],
        flops=2 * tokens * width * 4 * width,
        raw_in=range(1, 6),
        copies=5,
    )
    blocks_other = to_partner(blocks, inner)
    extra = -(-2 // (tokens // count)) * LANES
    back = call(
        functools.partial(norm_kernel, inner),
        sds((tokens, 2 * width + extra), BF),
        x,
        cot,
        gain,
        blocks,
        w_qkv,
        mixed,
        scratch=[vmem((tokens, 3 * width), BF), vmem((tokens, extra), F32)],
        flops=2 * tokens * width * 3 * width,
    )
    back = to_frames(back, count, held, patches).reshape(held * patches, -1)
    owned = sds((held * patches, width), BF)
    block_out, frames_grad, gain_grad = call(
        functools.partial(finish_kernel, inv_root),
        (owned, owned, sds((1, width // inner), F32)),
        frames.reshape(-1, width),
        w_out,
        back,
        flops=2 * tokens * width * width,
    )
    block_out, frames_grad = block_out.reshape(frames.shape), frames_grad.reshape(frames.shape)
    qkv_grad, out_grad = reduce_weights(mine, theirs, blocks, blocks_other, runs, inner, inv_root)
    return block_out, frames_grad, qkv_grad, out_grad, gain_grad.reshape(-1)


def solution(mesh):
    in_specs = (P(AXES, None, None), P(), P(), P(), P(AXES, None, None))
    out_specs = (P(AXES, None, None), P(AXES, None, None), P("inner", "tm"), P("inner", "tm"), P("inner"))
    return jax.shard_map(shards, mesh=mesh, in_specs=in_specs, out_specs=out_specs, check_vma=False)
```

```python
import functools
import math

import jax
import jax.numpy as jnp
from jax import lax
from jax.experimental import pallas as pl
from jax.experimental.pallas import tpu as pltpu
from jax.sharding import PartitionSpec as P


HEADS = 12
HEAD_DIM = 64
WINDOW = 4
CLIP_MAX = 256
EPSILON = 1e-06
SCALE = HEAD_DIM ** (-0.5)

BF = jnp.bfloat16
F32 = jnp.float32
AXES = ("tm", "inner")
LANES = 128
VMEM_SPARE = 8 * 1024 * 1024
PIECES = 2


def mm(a, b):
    return lax.dot_general(a, b, (((1,), (0,)), ((), ())), preferred_element_type=F32)


def mm_t(a, b):
    return lax.dot_general(a, b, (((1,), (1,)), ((), ())), preferred_element_type=F32)


def call(kernel, out_shape, *args, scratch=(), flops=0, raw_in=(), raw_out=(), copies=0, near_in=(), near_out=()):
    outs = jax.tree.leaves(out_shape)

    def size(arrays):
        return sum(math.prod(a.shape) * jnp.dtype(a.dtype).itemsize for a in arrays)

    def spec(raw):
        return pl.BlockSpec(memory_space=pltpu.HBM if raw else pltpu.VMEM)

    moved = size(outs) + size(args)
    out_specs = [spec(i in raw_out) for i in range(len(outs))]
    taken = size(a for i, a in enumerate(args) if i not in raw_in) + size(a for i, a in enumerate(outs) if i not in raw_out)
    semaphores = [pltpu.SemaphoreType.DMA((copies,))] if copies else []
    placed = [pltpu.HBM(a.shape, a.dtype) if i in raw_out else pltpu.VMEM(a.shape, a.dtype) if i in near_out else a for i, a in enumerate(outs)]
    args = [pltpu.with_memory_space_constraint(a, pltpu.HBM) if i in raw_in else pltpu.with_memory_space_constraint(a, pltpu.VMEM) if i in near_in else a for i, a in enumerate(args)]
    return pl.pallas_call(
        kernel,
        out_shape=placed if isinstance(out_shape, (tuple, list)) else placed[0],
        in_specs=[spec(i in raw_in) for i in range(len(args))],
        out_specs=out_specs if isinstance(out_shape, (tuple, list)) else out_specs[0],
        scratch_shapes=list(scratch) + semaphores,
        compiler_params=pltpu.CompilerParams(vmem_limit_bytes=taken + size(scratch) + VMEM_SPARE),
        cost_estimate=pl.CostEstimate(flops=flops, bytes_accessed=moved, transcendentals=0),
    )(*args)


def row_stats(x):
    center = x - jnp.mean(x, axis=-1, keepdims=True)
    spread = lax.rsqrt(jnp.mean(center * center, axis=-1, keepdims=True) + EPSILON)
    return center * spread, spread


def key_spans(tokens, reach):
    spans = []
    for start in range(0, tokens, LANES):
        low = max(0, start - reach) // 16 * 16
        high = min(tokens, -(-(start + LANES + reach) // 16) * 16)
        spans.append((start, low, high))
    return spans


def split_rows(mine_ref, other_ref, slot, src_ref, core):
    pieces, count, rows = mine_ref.shape[1:4]
    for z in range(count):
        for dst, which in ((mine_ref, core), (other_ref, 1 - core)):
            start = pl.multiple_of((2 * z + which) * pieces * rows, 8)
            block = src_ref[pl.ds(start, pieces * rows), :].astype(BF)
            for p in range(pieces):
                dst[slot, p, z] = block[p * rows : (p + 1) * rows]


def forward_kernel(reach, x_ref, gain_ref, bias_ref, wqkv_hbm, *rest):
    outs, (wqkv_ref, mine_ref, other_ref, q_ref, kt_ref, v_ref, prob_ref, mixed_ref, n_ref, k_ref, vt_ref, t_ref, weight_ref, sem) = rest[:7], rest[7:]
    tokens, width = x_ref.shape
    core = lax.axis_index("inner") & 1
    loads = []
    for part in range(3):
        cols = pl.ds(part * width, width)
        loads.append(pltpu.make_async_copy(wqkv_hbm.at[:, cols], wqkv_ref.at[part], sem.at[part]))
        loads[-1].start()
    sources = (mine_ref, other_ref, q_ref, kt_ref, v_ref, prob_ref, mixed_ref)
    stores = {i: pltpu.make_async_copy(sources[i], outs[i], sem.at[3 + i]) for i in (0, 1, 2, 3, 4, 6)}
    unit, _ = row_stats(x_ref[...].astype(F32))
    normed = unit * gain_ref[...]
    n_ref[...] = normed.astype(BF)
    t_ref[...] = normed.T
    split_rows(mine_ref, other_ref, 0, t_ref, core)
    step = 256
    for part, (dst, factor) in enumerate(((q_ref, SCALE), (k_ref, 1.0), (v_ref, 1.0))):
        loads[part].wait()
        for i in range(width // step):
            cols = slice(i * step, (i + 1) * step)
            dst[:, cols] = (mm(n_ref[...], wqkv_ref[part, :, cols]) * factor).astype(BF)
        if part != 1:
            stores[2 + part].start()

    def prob_store(i):
        heads = pl.ds(2 * i, 2)
        return pltpu.make_async_copy(prob_ref.at[heads], outs[5].at[heads], sem.at[10 + i])

    spans = key_spans(tokens, reach)
    for i in range(HEADS // 2):
        cols = slice(i * 128, i * 128 + 128)
        q2, k2 = q_ref[:, cols], k_ref[:, cols]
        kt_ref[cols, :] = (k2.astype(F32).T * SCALE).astype(BF)
        vt_ref[cols, :] = v_ref[:, cols].astype(F32).T.astype(BF)
        for half in range(2):
            span = slice(half * 64, half * 64 + 64)
            for b, (start, low, high) in enumerate(spans):
                block = slice(start, start + LANES)
                prob_ref[2 * i + half, b, : high - low] = mm_t(k2[low:high, span], q2[block, span])
    stores[3].start()
    for h in range(HEADS):
        for b, (start, low, high) in enumerate(spans):
            scores = prob_ref[h, b, : high - low] + bias_ref[low:high, start : start + LANES]
            grown = jnp.exp(scores - jnp.max(scores, axis=0, keepdims=True))
            probs = grown * (1.0 / jnp.sum(grown, axis=0, keepdims=True))
            prob_ref[h, b, : high - low] = probs
            weight_ref[h, b, : high - low] = probs.astype(BF)
        if h % 2:
            prob_store(h // 2).start()
    for h in range(HEADS):
        rows = slice(h * HEAD_DIM, (h + 1) * HEAD_DIM)
        for b, (start, low, high) in enumerate(spans):
            t_ref[rows, start : start + LANES] = mm(vt_ref[rows, :][:, low:high], weight_ref[h, b, : high - low])
    mixed_ref[...] = t_ref[...].T.astype(BF)
    stores[6].start()
    split_rows(mine_ref, other_ref, 1, t_ref, core)
    stores[0].start()
    stores[1].start()

    for i in range(HEADS // 2):
        prob_store(i).wait()
    for store in stores.values():
        store.wait()


def backward_kernel(reach, cot_ref, *rest):
    sources, blocks_ref, rest = rest[:5], rest[5], rest[6:]
    wout_ref, q_ref, kt_ref, v_ref, prob_ref, dqkv_ref, gm_ref, dqt_ref, dots_ref, grad_ref, weight_ref, sem = rest
    tokens, width = cot_ref.shape
    targets = (wout_ref, q_ref, kt_ref, v_ref, prob_ref)
    loads = [pltpu.make_async_copy(src, dst, sem.at[i]) for i, (src, dst) in enumerate(zip(sources, targets))]
    for load in loads:
        load.start()
    loads[0].wait()
    gm_ref[...] = mm_t(cot_ref[...], wout_ref[...]).astype(BF)
    for load in loads[1:]:
        load.wait()
    spans = key_spans(tokens, reach)

    for h in range(HEADS):
        cols = slice(h * HEAD_DIM, (h + 1) * HEAD_DIM)
        for b, (start, low, high) in enumerate(spans):
            dots_ref[h, b, : high - low] = mm_t(v_ref[low:high, cols], gm_ref[start : start + LANES, cols])
    for h in range(HEADS):
        for b, (start, low, high) in enumerate(spans):
            block = slice(start, start + LANES)
            probs, dots = prob_ref[h, b, : high - low], dots_ref[h, b, : high - low]
            centre = jnp.sum(probs * dots, axis=0, keepdims=True)
            for dst, value in ((grad_ref, probs * (dots - centre)), (weight_ref, probs)):
                dst[h, low:high, block] = value.astype(BF)
                if low:
                    dst[h, :low, block] = jnp.zeros((low, LANES), BF)
                if high < tokens:
                    dst[h, high:, block] = jnp.zeros((tokens - high, LANES), BF)
    for i in range(HEADS // 2):
        cols = slice(i * 128, i * 128 + 128)
        q2, g2 = q_ref[:, cols], gm_ref[:, cols]
        for at, source, right in ((1, grad_ref, q2), (2, weight_ref, g2)):
            pair = [mm(source[2 * i + half], right[:, half * 64 : half * 64 + 64]) for half in range(2)]
            dqkv_ref[:, at * width + i * 128 : at * width + i * 128 + 128] = jnp.concatenate(pair, 1).astype(BF)
        for h in (2 * i, 2 * i + 1):
            rows = slice(h * HEAD_DIM, (h + 1) * HEAD_DIM)
            dqt_ref[rows, :] = mm(kt_ref[rows, :], grad_ref[h])
    dqkv_ref[:, :width] = dqt_ref[...].T.astype(BF)
    runs = blocks_ref.shape[0]
    wide, thin = 3 * width // runs, width // runs
    for j in range(runs):
        blocks_ref[j, :, :wide] = dqkv_ref[:, j * wide : (j + 1) * wide]
        blocks_ref[j, :, wide:] = cot_ref[:, j * thin : (j + 1) * thin]


def norm_kernel(inner, x_ref, cot_ref, gain_ref, blocks_ref, wqkv_ref, mixed_ref, back_ref, dqkv_ref, extra_ref):
    tokens, width = x_ref.shape
    runs = blocks_ref.shape[0]
    wide = 3 * width // runs
    for j in range(runs):
        dqkv_ref[:, j * wide : (j + 1) * wide] = blocks_ref[j, :, :wide]
    unit, spread = row_stats(x_ref[...].astype(F32))
    ngrad = mm_t(dqkv_ref[...], wqkv_ref[...])
    part = jnp.sum(ngrad * unit, axis=0, keepdims=True)
    scaled = ngrad * gain_ref[...]
    mean_one = jnp.mean(scaled, axis=-1, keepdims=True)
    second = jnp.mean(scaled * unit, axis=-1, keepdims=True)
    back_ref[:, :width] = mixed_ref[...]
    back_ref[:, width : 2 * width] = (cot_ref[...].astype(F32) + spread * (scaled - mean_one - unit * second)).astype(BF)
    high = part.astype(BF).astype(F32)
    extra_ref[...] = jnp.zeros_like(extra_ref)
    share, each = width // inner, tokens // (runs * inner)
    for k, value in enumerate((high, part - high)):
        row, lane = k % each, k // each * LANES
        for i in range(inner):
            piece = value[:, i * share : (i + 1) * share]
            for t in range(runs):
                start = (t * inner + i) * each + row
                extra_ref[start : start + 1, lane : lane + share] = piece
    back_ref[:, 2 * width :] = extra_ref[...].astype(BF)


def finish_kernel(inv_root, frames_ref, wout_ref, back_ref, block_ref, fgrad_ref, gain_ref):
    width, share = fgrad_ref.shape[1], gain_ref.shape[1]
    block_ref[...] = (frames_ref[...].astype(F32) + mm(back_ref[:, :width], wout_ref[...])).astype(BF)
    fgrad_ref[...] = back_ref[:, width : 2 * width]
    total = jnp.sum(back_ref[:, 2 * width :].astype(F32), axis=0, keepdims=True)
    parts = [total[:, k : k + share] for k in range(0, total.shape[1], LANES)]
    gain_ref[...] = sum(parts) * inv_root


def squeeze_bits(value, bits):
    for b in sorted(bits, reverse=True):
        value = (value >> (b + 1) << b) | (value & ((1 << b) - 1))
    return value


def spread_bits(value, bits):
    for b in sorted(bits):
        value = (value >> b << (b + 1)) | (value & ((1 << b) - 1))
    return value


def bit_orders(runs):
    bits = list(range(runs.bit_length() - 1))
    return bits, bits[1:] + bits[:1]


def by_core(values):
    return jnp.where(lax.axis_index("inner") & 1 == 0, *values)


def run_of(runs, stage, n, send):
    me = lax.axis_index("tm")
    found = []
    for order in bit_orders(runs):
        past, bit = order[:stage], order[stage]
        run = spread_bits(n, past + [bit])
        for b in past:
            run = run | (me & (1 << b))
        found.append(run | ((me ^ (1 << bit) if send else me) & (1 << bit)))
    return by_core(found)


def place_of(runs, stage, run):
    return by_core([squeeze_bits(run, order[: stage + 1]) for order in bit_orders(runs)])


def exchange(value, runs, inner, stage):
    perm = []
    for t in range(runs):
        for i in range(inner):
            t2 = t ^ (1 << bit_orders(runs)[i & 1][stage])
            perm.append((t * inner + i, t2 * inner + i))
    return lax.ppermute(value, AXES, perm)


def to_partner(value, inner):
    return lax.ppermute(value, "inner", [(i, i ^ 1) for i in range(inner)])


def product_kernel(runs, pieces, send, mine_ref, other_ref, d_ref, d_other_ref, *out_refs):
    _, _, count, rows, tokens = mine_ref.shape
    for piece, out_ref in zip(pieces, out_refs):
        wide = out_ref.shape[3] * 3 // 4
        for n in range(out_ref.shape[0]):
            run = run_of(runs, 0, n, send)
            totals = []
            for slot, cols in ((0, slice(0, wide)), (1, slice(wide, None))):
                left = mine_ref[slot, piece].reshape(count * rows, tokens)
                right = other_ref[slot, piece].reshape(count * rows, tokens)
                totals.append(mm(left, d_ref[run, :, cols]) + mm(right, d_other_ref[run, :, cols]))
            total = jnp.concatenate(totals, 1).astype(out_ref.dtype)
            for z in range(count):
                out_ref[n, z] = total[z * rows : (z + 1) * rows]


def partial_sum(runs, run, keep_ref, got_refs, z):
    total = keep_ref[place_of(runs, 0, run), z]
    for stage, ref in enumerate(got_refs):
        total = total + ref[place_of(runs, stage, run), z].astype(F32)
    return total


def stage_kernel(runs, stage, keep_ref, *rest):
    got_refs, out_ref = rest[:-1], rest[-1]
    for n in range(out_ref.shape[0]):
        run = run_of(runs, stage, n, True)
        for z in range(out_ref.shape[1]):
            out_ref[n, z] = partial_sum(runs, run, keep_ref, got_refs, z).astype(BF)


def first_row_kernel(runs, keep_ref, *rest):
    got_refs, (send_ref, rest_ref) = rest[:-2], rest[-2:]
    me, run = lax.axis_index("inner") >> 1, lax.axis_index("tm")
    for n in range(send_ref.shape[0]):
        z = spread_bits(n, [0])
        rest_ref[n] = partial_sum(runs, run, keep_ref, got_refs, z | (me & 1))
        send_ref[n] = partial_sum(runs, run, keep_ref, got_refs, z | (1 - (me & 1))).astype(BF)


def row_kernel(stage, keep_ref, got_ref, send_ref, rest_ref):
    bit = (lax.axis_index("inner") >> (stage + 1)) & 1
    for n in range(send_ref.shape[0]):
        rest_ref[n] = keep_ref[2 * n + bit] + got_ref[2 * n + bit].astype(F32)
        other = 2 * n + 1 - bit
        send_ref[n] = (keep_ref[other] + got_ref[other].astype(F32)).astype(BF)


def last_kernel(inv_root, pieces, *rest):
    parts, (q_ref, o_ref) = rest[:-2], rest[-2:]
    rows, wide = q_ref.shape[0] // pieces, q_ref.shape[1]
    for p in range(pieces):
        total = (parts[2 * p][0] + parts[2 * p + 1][0].astype(F32)) * inv_root
        q_ref[p * rows : (p + 1) * rows] = total[:, :wide]
        o_ref[p * rows : (p + 1) * rows] = total[:, wide:]


def reduce_weights(mine, other, d, d_other, runs, inner, inv_root):
    sds = jax.ShapeDtypeStruct
    _, pieces, count, rows, tokens = mine.shape
    lanes = d.shape[2]
    stages = runs.bit_length() - 1
    shape = (runs // 2, count, rows, lanes)
    flops = 4 * count * rows * tokens * lanes * (runs // 2)
    args = (mine, other, d, d_other)

    def product(chosen, send, dtype):
        out = (sds(shape, dtype),) * len(chosen)
        return call(functools.partial(product_kernel, runs, chosen, send), out, *args, flops=len(chosen) * flops, near_in=range(4), near_out=range(2))

    got = [[] for _ in range(pieces)]
    for p in range(pieces):
        send = product((p,), True, BF)[0]
        got[p].append(exchange(send, runs, inner, 0))
    keep = list(product(tuple(range(pieces)), False, F32))
    for stage in range(1, stages):
        shape = (shape[0] // 2,) + shape[1:]
        for p in range(pieces):
            send = call(functools.partial(stage_kernel, runs, stage), sds(shape, BF), keep[p], *got[p])
            got[p].append(exchange(send, runs, inner, stage))
    for stage in range(count.bit_length() - 1):
        shape = (count >> (stage + 1), rows, lanes)
        out = (sds(shape, BF), sds(shape, F32))
        perm = [(i, i ^ (2 << stage)) for i in range(inner)]
        for p in range(pieces):
            body = functools.partial(row_kernel, stage) if stage else functools.partial(first_row_kernel, runs)
            send, keep[p] = call(body, out, keep[p], *got[p])
            got[p] = [lax.ppermute(send, "inner", perm)]
    last = []
    for p in range(pieces):
        last += [keep[p], *got[p]]
    out = (sds((pieces * rows, lanes * 3 // 4), F32), sds((pieces * rows, lanes // 4), F32))
    return call(functools.partial(last_kernel, inv_root, pieces), out, *last)


def to_tubes(rows, count):
    held, patches, width = rows.shape
    parts = jnp.moveaxis(rows.reshape(held, count, patches // count, width), 1, 0)
    parts = lax.all_to_all(parts, AXES, split_axis=0, concat_axis=0, tiled=True)
    return parts.reshape(-1, width)


def to_frames(tubes, count, held, patches):
    width = tubes.shape[1]
    parts = tubes.reshape(count, held, patches // count, width)
    parts = lax.all_to_all(parts, AXES, split_axis=0, concat_axis=0, tiled=True)
    return jnp.moveaxis(parts, 0, 1).reshape(held, patches, width)


def window_bias(all_frames, patches, clip_len):
    tokens = all_frames * patches
    key = lax.broadcasted_iota(jnp.int32, (tokens, tokens), 0)
    query = lax.broadcasted_iota(jnp.int32, (tokens, tokens), 1)
    key_f, query_f = key // patches, query // patches
    inside = (key % patches == query % patches) & (abs(key_f - query_f) <= WINDOW)
    inside = inside & (key_f // clip_len == query_f // clip_len)
    return jnp.where(inside, 0.0, -1e30).astype(F32)


def attend(x, gain, w_qkv, bias, reach, inner):
    tokens, width = x.shape
    spans = key_spans(tokens, reach)
    longest = max(high - low for _, low, high in spans)
    sds, vmem = jax.ShapeDtypeStruct, pltpu.VMEM
    halves = ((2, PIECES, inner // 2, width // inner // PIECES, tokens), BF)
    flat, turned = ((tokens, width), BF), ((width, tokens), BF)
    probs = ((HEADS, len(spans), longest, LANES), F32)
    made = (halves, halves, flat, turned, flat, probs, flat)
    return call(
        functools.partial(forward_kernel, reach),
        tuple(sds(*each) for each in made),
        x,
        gain,
        bias,
        w_qkv,
        scratch=[vmem((3, width, width), BF), *(vmem(*each) for each in made), vmem(*flat), vmem(*flat), vmem(*turned), vmem((width, tokens), F32), vmem(probs[0], BF)],
        flops=2 * tokens * width * 4 * width,
        raw_in=(3,),
        raw_out=range(7),
        copies=10 + HEADS // 2,
    )


def attend_back(cot, w_out, q, kt, v, prob, reach, runs):
    tokens, width = cot.shape
    sds, vmem = jax.ShapeDtypeStruct, pltpu.VMEM
    flat, turned, probs = (q.shape, BF), (kt.shape, BF), (prob.shape, F32)
    made = ((runs, tokens, 4 * width // runs), BF)
    return call(
        functools.partial(backward_kernel, reach),
        sds(*made),
        cot,
        w_out,
        q,
        kt,
        v,
        prob,
        scratch=[*(vmem(*each) for each in (((width, width), BF), flat, turned, flat, probs)), vmem((tokens, 3 * width), BF), vmem(*flat), vmem((width, tokens), F32), vmem(*probs), vmem((HEADS, tokens, tokens), BF), vmem((HEADS, tokens, tokens), BF)],
        flops=2 * tokens * width * 4 * width,
        raw_in=range(1, 6),
        copies=5,
    )


def shards(frames, norm_gain, w_qkv, w_out, cotangent):
    held, patches, width = frames.shape
    runs, inner = lax.axis_size("tm"), lax.axis_size("inner")
    count = runs * inner
    all_frames = held * count
    clip_len = min(CLIP_MAX, all_frames)
    inv_root = 1.0 / math.sqrt(all_frames * patches)
    tokens = all_frames * patches // count
    reach = WINDOW * (patches // count)
    gain = norm_gain.reshape(1, width)
    bias = window_bias(all_frames, patches // count, clip_len)
    spans = key_spans(tokens, reach)
    longest = max(high - low for _, low, high in spans)
    sds = jax.ShapeDtypeStruct
    vmem = pltpu.VMEM

    x = to_tubes(frames, count)
    cot = to_tubes(cotangent, count)
    mine, other, q, kt, v, prob, mixed = attend(x, gain, w_qkv, bias, reach, inner)
    theirs = to_partner(other, inner)
    blocks = attend_back(cot, w_out, q, kt, v, prob, reach, runs)
    blocks_other = to_partner(blocks, inner)
    extra = -(-2 // (tokens // count)) * LANES
    back = call(
        functools.partial(norm_kernel, inner),
        sds((tokens, 2 * width + extra), BF),
        x,
        cot,
        gain,
        blocks,
        w_qkv,
        mixed,
        scratch=[vmem((tokens, 3 * width), BF), vmem((tokens, extra), F32)],
        flops=2 * tokens * width * 3 * width,
    )
    back = to_frames(back, count, held, patches).reshape(held * patches, -1)
    owned = sds((held * patches, width), BF)
    block_out, frames_grad, gain_grad = call(
        functools.partial(finish_kernel, inv_root),
        (owned, owned, sds((1, width // inner), F32)),
        frames.reshape(-1, width),
        w_out,
        back,
        flops=2 * tokens * width * width,
    )
    block_out, frames_grad = block_out.reshape(frames.shape), frames_grad.reshape(frames.shape)
    qkv_grad, out_grad = reduce_weights(mine, theirs, blocks, blocks_other, runs, inner, inv_root)
    return block_out, frames_grad, qkv_grad, out_grad, gain_grad.reshape(-1)


def solution(mesh):
    in_specs = (P(AXES, None, None), P(), P(), P(), P(AXES, None, None))
    out_specs = (P(AXES, None, None), P(AXES, None, None), P("inner", "tm"), P("inner", "tm"), P("inner"))
    return jax.shard_map(shards, mesh=mesh, in_specs=in_specs, out_specs=out_specs, check_vma=False)
```

```python
import functools
import math

import jax
import jax.numpy as jnp
from jax import lax
from jax.experimental import pallas as pl
from jax.experimental.pallas import tpu as pltpu
from jax.sharding import PartitionSpec as P


HEADS = 12
HEAD_DIM = 64
WINDOW = 4
CLIP_MAX = 256
EPSILON = 1e-06
SCALE = HEAD_DIM ** (-0.5)

BF = jnp.bfloat16
F32 = jnp.float32
AXES = ("tm", "inner")
LANES = 128
VMEM_SPARE = 8 * 1024 * 1024


def mm(a, b):
    return lax.dot_general(a, b, (((1,), (0,)), ((), ())), preferred_element_type=F32)


def mm_t(a, b):
    return lax.dot_general(a, b, (((1,), (1,)), ((), ())), preferred_element_type=F32)


def call(kernel, out_shape, *args, scratch=(), flops=0, raw_in=(), raw_out=(), copies=0, near_in=(), near_out=()):
    outs = jax.tree.leaves(out_shape)

    def size(arrays):
        return sum(math.prod(a.shape) * jnp.dtype(a.dtype).itemsize for a in arrays)

    def spec(raw):
        return pl.BlockSpec(memory_space=pltpu.HBM if raw else pltpu.VMEM)

    moved = size(outs) + size(args)
    out_specs = [spec(i in raw_out) for i in range(len(outs))]
    taken = size(a for i, a in enumerate(args) if i not in raw_in) + size(a for i, a in enumerate(outs) if i not in raw_out)
    semaphores = [pltpu.SemaphoreType.DMA((copies,))] if copies else []
    placed = [pltpu.HBM(a.shape, a.dtype) if i in raw_out else pltpu.VMEM(a.shape, a.dtype) if i in near_out else a for i, a in enumerate(outs)]
    args = [pltpu.with_memory_space_constraint(a, pltpu.HBM) if i in raw_in else pltpu.with_memory_space_constraint(a, pltpu.VMEM) if i in near_in else a for i, a in enumerate(args)]
    return pl.pallas_call(
        kernel,
        out_shape=placed if isinstance(out_shape, (tuple, list)) else placed[0],
        in_specs=[spec(i in raw_in) for i in range(len(args))],
        out_specs=out_specs if isinstance(out_shape, (tuple, list)) else out_specs[0],
        scratch_shapes=list(scratch) + semaphores,
        compiler_params=pltpu.CompilerParams(vmem_limit_bytes=taken + size(scratch) + VMEM_SPARE),
        cost_estimate=pl.CostEstimate(flops=flops, bytes_accessed=moved, transcendentals=0),
    )(*args)


def row_stats(x):
    center = x - jnp.mean(x, axis=-1, keepdims=True)
    spread = lax.rsqrt(jnp.mean(center * center, axis=-1, keepdims=True) + EPSILON)
    return center * spread, spread


def key_spans(tokens, reach):
    spans = []
    for start in range(0, tokens, LANES):
        low = max(0, start - reach) // 16 * 16
        high = min(tokens, -(-(start + LANES + reach) // 16) * 16)
        spans.append((start, low, high))
    return spans


def split_rows(mine_ref, other_ref, slot, src_ref, core):
    count, rows = mine_ref.shape[1:3]
    for z in range(count):
        for dst, which in ((mine_ref, core), (other_ref, 1 - core)):
            start = pl.multiple_of((2 * z + which) * rows, 8)
            dst[slot, z] = src_ref[pl.ds(start, rows), :].astype(BF)


def forward_kernel(reach, x_ref, gain_ref, bias_ref, wqkv_hbm, *rest):
    outs, (wqkv_ref, mine_ref, other_ref, q_ref, kt_ref, v_ref, prob_ref, mixed_ref, n_ref, k_ref, vt_ref, t_ref, weight_ref, sem) = rest[:7], rest[7:]
    tokens, width = x_ref.shape
    core = lax.axis_index("inner") & 1
    loads = []
    for part in range(3):
        cols = pl.ds(part * width, width)
        loads.append(pltpu.make_async_copy(wqkv_hbm.at[:, cols], wqkv_ref.at[part], sem.at[part]))
        loads[-1].start()
    sources = (mine_ref, other_ref, q_ref, kt_ref, v_ref, prob_ref, mixed_ref)
    stores = {i: pltpu.make_async_copy(sources[i], outs[i], sem.at[3 + i]) for i in (0, 1, 2, 3, 4, 6)}
    unit, _ = row_stats(x_ref[...].astype(F32))
    normed = unit * gain_ref[...]
    n_ref[...] = normed.astype(BF)
    t_ref[...] = normed.T
    split_rows(mine_ref, other_ref, 0, t_ref, core)
    step = 256
    for part, (dst, factor) in enumerate(((q_ref, SCALE), (k_ref, 1.0), (v_ref, 1.0))):
        loads[part].wait()
        for i in range(width // step):
            cols = slice(i * step, (i + 1) * step)
            dst[:, cols] = (mm(n_ref[...], wqkv_ref[part, :, cols]) * factor).astype(BF)
        if part != 1:
            stores[2 + part].start()

    def prob_store(i):
        heads = pl.ds(2 * i, 2)
        return pltpu.make_async_copy(prob_ref.at[heads], outs[5].at[heads], sem.at[10 + i])

    spans = key_spans(tokens, reach)
    for i in range(HEADS // 2):
        cols = slice(i * 128, i * 128 + 128)
        q2, k2 = q_ref[:, cols], k_ref[:, cols]
        kt_ref[cols, :] = (k2.astype(F32).T * SCALE).astype(BF)
        vt_ref[cols, :] = v_ref[:, cols].astype(F32).T.astype(BF)
        for half in range(2):
            span = slice(half * 64, half * 64 + 64)
            for b, (start, low, high) in enumerate(spans):
                block = slice(start, start + LANES)
                prob_ref[2 * i + half, b, : high - low] = mm_t(k2[low:high, span], q2[block, span])
    stores[3].start()
    for h in range(HEADS):
        for b, (start, low, high) in enumerate(spans):
            scores = prob_ref[h, b, : high - low] + bias_ref[low:high, start : start + LANES]
            grown = jnp.exp(scores - jnp.max(scores, axis=0, keepdims=True))
            probs = grown * (1.0 / jnp.sum(grown, axis=0, keepdims=True))
            prob_ref[h, b, : high - low] = probs
            weight_ref[h, b, : high - low] = probs.astype(BF)
        if h % 2:
            prob_store(h // 2).start()
    for h in range(HEADS):
        rows = slice(h * HEAD_DIM, (h + 1) * HEAD_DIM)
        for b, (start, low, high) in enumerate(spans):
            t_ref[rows, start : start + LANES] = mm(vt_ref[rows, :][:, low:high], weight_ref[h, b, : high - low])
    mixed_ref[...] = t_ref[...].T.astype(BF)
    stores[6].start()
    split_rows(mine_ref, other_ref, 1, t_ref, core)
    stores[0].start()
    stores[1].start()

    for i in range(HEADS // 2):
        prob_store(i).wait()
    for store in stores.values():
        store.wait()


def backward_kernel(reach, cot_ref, *rest):
    sources, blocks_ref, rest = rest[:5], rest[5], rest[6:]
    wout_ref, q_ref, kt_ref, v_ref, prob_ref, dqkv_ref, gm_ref, dqt_ref, dots_ref, grad_ref, weight_ref, sem = rest
    tokens, width = cot_ref.shape
    targets = (wout_ref, q_ref, kt_ref, v_ref, prob_ref)
    loads = [pltpu.make_async_copy(src, dst, sem.at[i]) for i, (src, dst) in enumerate(zip(sources, targets))]
    for load in loads:
        load.start()
    loads[0].wait()
    gm_ref[...] = mm_t(cot_ref[...], wout_ref[...]).astype(BF)
    for load in loads[1:]:
        load.wait()
    spans = key_spans(tokens, reach)

    for h in range(HEADS):
        cols = slice(h * HEAD_DIM, (h + 1) * HEAD_DIM)
        for b, (start, low, high) in enumerate(spans):
            dots_ref[h, b, : high - low] = mm_t(v_ref[low:high, cols], gm_ref[start : start + LANES, cols])
    for h in range(HEADS):
        for b, (start, low, high) in enumerate(spans):
            block = slice(start, start + LANES)
            probs, dots = prob_ref[h, b, : high - low], dots_ref[h, b, : high - low]
            centre = jnp.sum(probs * dots, axis=0, keepdims=True)
            for dst, value in ((grad_ref, probs * (dots - centre)), (weight_ref, probs)):
                dst[h, low:high, block] = value.astype(BF)
                if low:
                    dst[h, :low, block] = jnp.zeros((low, LANES), BF)
                if high < tokens:
                    dst[h, high:, block] = jnp.zeros((tokens - high, LANES), BF)
    for i in range(HEADS // 2):
        cols = slice(i * 128, i * 128 + 128)
        q2, g2 = q_ref[:, cols], gm_ref[:, cols]
        for at, source, right in ((1, grad_ref, q2), (2, weight_ref, g2)):
            pair = [mm(source[2 * i + half], right[:, half * 64 : half * 64 + 64]) for half in range(2)]
            dqkv_ref[:, at * width + i * 128 : at * width + i * 128 + 128] = jnp.concatenate(pair, 1).astype(BF)
        for h in (2 * i, 2 * i + 1):
            rows = slice(h * HEAD_DIM, (h + 1) * HEAD_DIM)
            dqt_ref[rows, :] = mm(kt_ref[rows, :], grad_ref[h])
    dqkv_ref[:, :width] = dqt_ref[...].T.astype(BF)
    runs = blocks_ref.shape[0]
    wide, thin = 3 * width // runs, width // runs
    for j in range(runs):
        blocks_ref[j, :, :wide] = dqkv_ref[:, j * wide : (j + 1) * wide]
        blocks_ref[j, :, wide:] = cot_ref[:, j * thin : (j + 1) * thin]


def norm_kernel(inner, x_ref, cot_ref, gain_ref, blocks_ref, wqkv_ref, mixed_ref, back_ref, dqkv_ref, extra_ref):
    tokens, width = x_ref.shape
    runs = blocks_ref.shape[0]
    wide = 3 * width // runs
    for j in range(runs):
        dqkv_ref[:, j * wide : (j + 1) * wide] = blocks_ref[j, :, :wide]
    unit, spread = row_stats(x_ref[...].astype(F32))
    ngrad = mm_t(dqkv_ref[...], wqkv_ref[...])
    part = jnp.sum(ngrad * unit, axis=0, keepdims=True)
    scaled = ngrad * gain_ref[...]
    mean_one = jnp.mean(scaled, axis=-1, keepdims=True)
    second = jnp.mean(scaled * unit, axis=-1, keepdims=True)
    back_ref[:, :width] = mixed_ref[...]
    back_ref[:, width : 2 * width] = (cot_ref[...].astype(F32) + spread * (scaled - mean_one - unit * second)).astype(BF)
    high = part.astype(BF).astype(F32)
    extra_ref[...] = jnp.zeros_like(extra_ref)
    share, each = width // inner, tokens // (runs * inner)
    for k, value in enumerate((high, part - high)):
        row, lane = k % each, k // each * LANES
        for i in range(inner):
            piece = value[:, i * share : (i + 1) * share]
            for t in range(runs):
                start = (t * inner + i) * each + row
                extra_ref[start : start + 1, lane : lane + share] = piece
    back_ref[:, 2 * width :] = extra_ref[...].astype(BF)


def finish_kernel(inv_root, frames_ref, wout_ref, back_ref, block_ref, fgrad_ref, gain_ref):
    width, share = fgrad_ref.shape[1], gain_ref.shape[1]
    block_ref[...] = (frames_ref[...].astype(F32) + mm(back_ref[:, :width], wout_ref[...])).astype(BF)
    fgrad_ref[...] = back_ref[:, width : 2 * width]
    total = jnp.sum(back_ref[:, 2 * width :].astype(F32), axis=0, keepdims=True)
    parts = [total[:, k : k + share] for k in range(0, total.shape[1], LANES)]
    gain_ref[...] = sum(parts) * inv_root


def squeeze_bits(value, bits):
    for b in sorted(bits, reverse=True):
        value = (value >> (b + 1) << b) | (value & ((1 << b) - 1))
    return value


def spread_bits(value, bits):
    for b in sorted(bits):
        value = (value >> b << (b + 1)) | (value & ((1 << b) - 1))
    return value


def bit_orders(runs):
    bits = list(range(runs.bit_length() - 1))
    return bits, bits[1:] + bits[:1]


def by_core(values):
    return jnp.where(lax.axis_index("inner") & 1 == 0, *values)


def run_of(runs, stage, n, send):
    me = lax.axis_index("tm")
    found = []
    for order in bit_orders(runs):
        past, bit = order[:stage], order[stage]
        run = spread_bits(n, past + [bit])
        for b in past:
            run = run | (me & (1 << b))
        found.append(run | ((me ^ (1 << bit) if send else me) & (1 << bit)))
    return by_core(found)


def place_of(runs, stage, run):
    return by_core([squeeze_bits(run, order[: stage + 1]) for order in bit_orders(runs)])


def exchange(value, runs, inner, stage):
    perm = []
    for t in range(runs):
        for i in range(inner):
            t2 = t ^ (1 << bit_orders(runs)[i & 1][stage])
            perm.append((t * inner + i, t2 * inner + i))
    return lax.ppermute(value, AXES, perm)


def to_partner(value, inner):
    return lax.ppermute(value, "inner", [(i, i ^ 1) for i in range(inner)])


def pieces_of(rows):
    cut = rows // 2
    return ((0, cut), (cut, rows))


def product_kernel(pieces, choose, mine_ref, other_ref, d_ref, d_other_ref, *out_refs):
    _, count, _, tokens = mine_ref.shape
    for index, (low, high) in enumerate(pieces):
        refs = out_refs[index * len(out_refs) // len(pieces) : (index + 1) * len(out_refs) // len(pieces)]
        wide = d_ref.shape[2] * 3 // 4
        for out_ref, runs in zip(refs, choose()):
            for n, run in enumerate(runs):
                totals = []
                for slot, cols in ((0, slice(0, wide)), (1, slice(wide, None))):
                    left = mine_ref[slot, :, low:high].reshape(count * (high - low), tokens)
                    right = other_ref[slot, :, low:high].reshape(count * (high - low), tokens)
                    totals.append(mm(left, d_ref[run, :, cols]) + mm(right, d_other_ref[run, :, cols]))
                total = jnp.concatenate(totals, 1).astype(out_ref.dtype)
                for z in range(count):
                    out_ref[n, z] = total[z * (high - low) : (z + 1) * (high - low)]


def partial_sum(runs, run, own_ref, n, got_refs, z):
    total = own_ref[n, z]
    for stage, ref in enumerate(got_refs):
        total = total + ref[place_of(runs, stage, run), z].astype(F32)
    return total


def stage_kernel(runs, stage, own_ref, *rest):
    got_refs, out_ref = rest[:-1], rest[-1]
    for n in range(out_ref.shape[0]):
        run = run_of(runs, stage, n, True)
        for z in range(out_ref.shape[1]):
            out_ref[n, z] = partial_sum(runs, run, own_ref, n, got_refs, z).astype(BF)


def first_row_kernel(runs, own_ref, *rest):
    got_refs, (send_ref, rest_ref) = rest[:-2], rest[-2:]
    me, run = lax.axis_index("inner") >> 1, lax.axis_index("tm")
    for n in range(send_ref.shape[0]):
        z = spread_bits(n, [0])
        rest_ref[n] = partial_sum(runs, run, own_ref, 0, got_refs, z | (me & 1))
        send_ref[n] = partial_sum(runs, run, own_ref, 0, got_refs, z | (1 - (me & 1))).astype(BF)


def row_kernel(stage, keep_ref, got_ref, send_ref, rest_ref):
    bit = (lax.axis_index("inner") >> (stage + 1)) & 1
    for n in range(send_ref.shape[0]):
        rest_ref[n] = keep_ref[2 * n + bit] + got_ref[2 * n + bit].astype(F32)
        other = 2 * n + 1 - bit
        send_ref[n] = (keep_ref[other] + got_ref[other].astype(F32)).astype(BF)


def last_kernel(inv_root, *rest):
    parts, (q_ref, o_ref) = rest[:-2], rest[-2:]
    wide = q_ref.shape[1]
    for p, (low, high) in enumerate(pieces_of(q_ref.shape[0])):
        total = (parts[2 * p][0] + parts[2 * p + 1][0].astype(F32)) * inv_root
        q_ref[low:high] = total[:, :wide]
        o_ref[low:high] = total[:, wide:]


def reduce_weights(mine, other, d, d_other, runs, inner, inv_root):
    sds = jax.ShapeDtypeStruct
    _, count, rows, tokens = mine.shape
    lanes = d.shape[2]
    stages = runs.bit_length() - 1
    pieces = pieces_of(rows)
    args = (mine, other, d, d_other)

    def wanted(stage):
        if stage == stages:
            return [lax.axis_index("tm")]
        return [run_of(runs, stage, n, True) for n in range(runs >> (stage + 1))]

    def product(chosen, which, dtype):
        shapes = [(max(runs >> (stage + 1), 1), count, high - low, lanes) for low, high in chosen for stage in which]
        flops = sum(4 * math.prod(shape) * tokens for shape in shapes)
        body = functools.partial(product_kernel, chosen, lambda: [wanted(stage) for stage in which])
        return call(body, tuple(sds(shape, dtype) for shape in shapes), *args, flops=flops, near_in=range(4), near_out=range(len(shapes)))

    got = [[] for _ in pieces]
    for p, piece in enumerate(pieces):
        send = product((piece,), (0,), BF)[0]
        got[p].append(exchange(send, runs, inner, 0))
    later = product(pieces, tuple(range(1, stages + 1)), F32)
    own = [later[p * stages : (p + 1) * stages] for p in range(len(pieces))]
    for stage in range(1, stages):
        for p in range(len(pieces)):
            body = functools.partial(stage_kernel, runs, stage)
            send = call(body, sds(own[p][stage - 1].shape, BF), own[p][stage - 1], *got[p])
            got[p].append(exchange(send, runs, inner, stage))
    keep = [each[-1] for each in own]
    for stage in range(count.bit_length() - 1):
        perm = [(i, i ^ (2 << stage)) for i in range(inner)]
        for p, (low, high) in enumerate(pieces):
            shape = (count >> (stage + 1), high - low, lanes)
            body = functools.partial(row_kernel, stage) if stage else functools.partial(first_row_kernel, runs)
            send, keep[p] = call(body, (sds(shape, BF), sds(shape, F32)), keep[p], *got[p])
            got[p] = [lax.ppermute(send, "inner", perm)]
    last = []
    for p in range(len(pieces)):
        last += [keep[p], *got[p]]
    out = (sds((rows, lanes * 3 // 4), F32), sds((rows, lanes // 4), F32))
    return call(functools.partial(last_kernel, inv_root), out, *last)


def to_tubes(rows, count):
    held, patches, width = rows.shape
    parts = jnp.moveaxis(rows.reshape(held, count, patches // count, width), 1, 0)
    parts = lax.all_to_all(parts, AXES, split_axis=0, concat_axis=0, tiled=True)
    return parts.reshape(-1, width)


def to_frames(tubes, count, held, patches):
    width = tubes.shape[1]
    parts = tubes.reshape(count, held, patches // count, width)
    parts = lax.all_to_all(parts, AXES, split_axis=0, concat_axis=0, tiled=True)
    return jnp.moveaxis(parts, 0, 1).reshape(held, patches, width)


def window_bias(all_frames, patches, clip_len):
    tokens = all_frames * patches
    key = lax.broadcasted_iota(jnp.int32, (tokens, tokens), 0)
    query = lax.broadcasted_iota(jnp.int32, (tokens, tokens), 1)
    key_f, query_f = key // patches, query // patches
    inside = (key % patches == query % patches) & (abs(key_f - query_f) <= WINDOW)
    inside = inside & (key_f // clip_len == query_f // clip_len)
    return jnp.where(inside, 0.0, -1e30).astype(F32)


def attend(x, gain, w_qkv, bias, reach, inner):
    tokens, width = x.shape
    spans = key_spans(tokens, reach)
    longest = max(high - low for _, low, high in spans)
    sds, vmem = jax.ShapeDtypeStruct, pltpu.VMEM
    halves = ((2, inner // 2, width // inner, tokens), BF)
    flat, turned = ((tokens, width), BF), ((width, tokens), BF)
    probs = ((HEADS, len(spans), longest, LANES), F32)
    made = (halves, halves, flat, turned, flat, probs, flat)
    return call(
        functools.partial(forward_kernel, reach),
        tuple(sds(*each) for each in made),
        x,
        gain,
        bias,
        w_qkv,
        scratch=[vmem((3, width, width), BF), *(vmem(*each) for each in made), vmem(*flat), vmem(*flat), vmem(*turned), vmem((width, tokens), F32), vmem(probs[0], BF)],
        flops=2 * tokens * width * 4 * width,
        raw_in=(3,),
        raw_out=range(7),
        copies=10 + HEADS // 2,
    )


def attend_back(cot, w_out, q, kt, v, prob, reach, runs):
    tokens, width = cot.shape
    sds, vmem = jax.ShapeDtypeStruct, pltpu.VMEM
    flat, turned, probs = (q.shape, BF), (kt.shape, BF), (prob.shape, F32)
    made = ((runs, tokens, 4 * width // runs), BF)
    return call(
        functools.partial(backward_kernel, reach),
        sds(*made),
        cot,
        w_out,
        q,
        kt,
        v,
        prob,
        scratch=[*(vmem(*each) for each in (((width, width), BF), flat, turned, flat, probs)), vmem((tokens, 3 * width), BF), vmem(*flat), vmem((width, tokens), F32), vmem(*probs), vmem((HEADS, tokens, tokens), BF), vmem((HEADS, tokens, tokens), BF)],
        flops=2 * tokens * width * 4 * width,
        raw_in=range(1, 6),
        copies=5,
    )


def shards(frames, norm_gain, w_qkv, w_out, cotangent):
    held, patches, width = frames.shape
    runs, inner = lax.axis_size("tm"), lax.axis_size("inner")
    count = runs * inner
    all_frames = held * count
    clip_len = min(CLIP_MAX, all_frames)
    inv_root = 1.0 / math.sqrt(all_frames * patches)
    tokens = all_frames * patches // count
    reach = WINDOW * (patches // count)
    gain = norm_gain.reshape(1, width)
    bias = window_bias(all_frames, patches // count, clip_len)
    spans = key_spans(tokens, reach)
    longest = max(high - low for _, low, high in spans)
    sds = jax.ShapeDtypeStruct
    vmem = pltpu.VMEM

    x = to_tubes(frames, count)
    cot = to_tubes(cotangent, count)
    mine, other, q, kt, v, prob, mixed = attend(x, gain, w_qkv, bias, reach, inner)
    theirs = to_partner(other, inner)
    blocks = attend_back(cot, w_out, q, kt, v, prob, reach, runs)
    blocks_other = to_partner(blocks, inner)
    extra = -(-2 // (tokens // count)) * LANES
    back = call(
        functools.partial(norm_kernel, inner),
        sds((tokens, 2 * width + extra), BF),
        x,
        cot,
        gain,
        blocks,
        w_qkv,
        mixed,
        scratch=[vmem((tokens, 3 * width), BF), vmem((tokens, extra), F32)],
        flops=2 * tokens * width * 3 * width,
    )
    back = to_frames(back, count, held, patches).reshape(held * patches, -1)
    owned = sds((held * patches, width), BF)
    block_out, frames_grad, gain_grad = call(
        functools.partial(finish_kernel, inv_root),
        (owned, owned, sds((1, width // inner), F32)),
        frames.reshape(-1, width),
        w_out,
        back,
        flops=2 * tokens * width * width,
    )
    block_out, frames_grad = block_out.reshape(frames.shape), frames_grad.reshape(frames.shape)
    qkv_grad, out_grad = reduce_weights(mine, theirs, blocks, blocks_other, runs, inner, inv_root)
    return block_out, frames_grad, qkv_grad, out_grad, gain_grad.reshape(-1)


def solution(mesh):
    in_specs = (P(AXES, None, None), P(), P(), P(), P(AXES, None, None))
    out_specs = (P(AXES, None, None), P(AXES, None, None), P("inner", "tm"), P("inner", "tm"), P("inner"))
    return jax.shard_map(shards, mesh=mesh, in_specs=in_specs, out_specs=out_specs, check_vma=False)
```

```python
import functools
import math

import jax
import jax.numpy as jnp
from jax import lax
from jax.experimental import pallas as pl
from jax.experimental.pallas import tpu as pltpu
from jax.sharding import PartitionSpec as P


HEADS = 12
HEAD_DIM = 64
WINDOW = 4
CLIP_MAX = 256
EPSILON = 1e-06
SCALE = HEAD_DIM ** (-0.5)

BF = jnp.bfloat16
F32 = jnp.float32
AXES = ("tm", "inner")
LANES = 128
VMEM_SPARE = 8 * 1024 * 1024
DIRECT_FROM = 1
PARTS = 2


def mm(a, b):
    return lax.dot_general(a, b, (((1,), (0,)), ((), ())), preferred_element_type=F32)


def mm_t(a, b):
    return lax.dot_general(a, b, (((1,), (1,)), ((), ())), preferred_element_type=F32)


def call(kernel, out_shape, *args, scratch=(), flops=0, raw_in=(), raw_out=(), copies=0, near_in=(), near_out=(), far_out=False):
    outs = jax.tree.leaves(out_shape)

    def size(arrays):
        return sum(math.prod(a.shape) * jnp.dtype(a.dtype).itemsize for a in arrays)

    def spec(raw):
        return pl.BlockSpec(memory_space=pltpu.HBM if raw else pltpu.VMEM)

    moved = size(outs) + size(args)
    out_specs = [spec(i in raw_out) for i in range(len(outs))]
    taken = size(a for i, a in enumerate(args) if i not in raw_in) + size(a for i, a in enumerate(outs) if i not in raw_out)
    semaphores = [pltpu.SemaphoreType.DMA((copies,))] if copies else []
    placed = [pltpu.HBM(a.shape, a.dtype) if i in raw_out or far_out else pltpu.VMEM(a.shape, a.dtype) if i in near_out else a for i, a in enumerate(outs)]
    args = [pltpu.with_memory_space_constraint(a, pltpu.HBM) if i in raw_in else pltpu.with_memory_space_constraint(a, pltpu.VMEM) if i in near_in else a for i, a in enumerate(args)]
    return pl.pallas_call(
        kernel,
        out_shape=placed if isinstance(out_shape, (tuple, list)) else placed[0],
        in_specs=[spec(i in raw_in) for i in range(len(args))],
        out_specs=out_specs if isinstance(out_shape, (tuple, list)) else out_specs[0],
        scratch_shapes=list(scratch) + semaphores,
        compiler_params=pltpu.CompilerParams(vmem_limit_bytes=taken + size(scratch) + VMEM_SPARE),
        cost_estimate=pl.CostEstimate(flops=flops, bytes_accessed=moved, transcendentals=0),
    )(*args)


def row_stats(x):
    center = x - jnp.mean(x, axis=-1, keepdims=True)
    spread = lax.rsqrt(jnp.mean(center * center, axis=-1, keepdims=True) + EPSILON)
    return center * spread, spread


def key_spans(tokens, reach):
    spans = []
    for start in range(0, tokens, LANES):
        low = max(0, start - reach) // 16 * 16
        high = min(tokens, -(-(start + LANES + reach) // 16) * 16)
        spans.append((start, low, high))
    return spans


def split_rows(mine_ref, other_ref, slot, src_ref, core):
    count, rows = mine_ref.shape[1:3]
    for z in range(count):
        for dst, which in ((mine_ref, core), (other_ref, 1 - core)):
            start = pl.multiple_of((2 * z + which) * rows, 8)
            dst[slot, z] = src_ref[pl.ds(start, rows), :].astype(BF)


def forward_kernel(reach, x_ref, gain_ref, bias_ref, wqkv_hbm, *rest):
    outs, (wqkv_ref, mine_ref, other_ref, q_ref, kt_ref, v_ref, prob_ref, mixed_ref, n_ref, k_ref, vt_ref, t_ref, weight_ref, sem) = rest[:7], rest[7:]
    tokens, width = x_ref.shape
    core = lax.axis_index("inner") & 1
    loads = []
    for part in range(3):
        cols = pl.ds(part * width, width)
        loads.append(pltpu.make_async_copy(wqkv_hbm.at[:, cols], wqkv_ref.at[part], sem.at[part]))
        loads[-1].start()
    sources = (mine_ref, other_ref, q_ref, kt_ref, v_ref, prob_ref, mixed_ref)
    stores = {i: pltpu.make_async_copy(sources[i], outs[i], sem.at[3 + i]) for i in (0, 1, 2, 3, 4, 6)}
    unit, _ = row_stats(x_ref[...].astype(F32))
    normed = unit * gain_ref[...]
    n_ref[...] = normed.astype(BF)
    t_ref[...] = normed.T
    split_rows(mine_ref, other_ref, 0, t_ref, core)
    step = 256
    for part, (dst, factor) in enumerate(((q_ref, SCALE), (k_ref, 1.0), (v_ref, 1.0))):
        loads[part].wait()
        for i in range(width // step):
            cols = slice(i * step, (i + 1) * step)
            dst[:, cols] = (mm(n_ref[...], wqkv_ref[part, :, cols]) * factor).astype(BF)
        if part != 1:
            stores[2 + part].start()

    def prob_store(i):
        heads = pl.ds(2 * i, 2)
        return pltpu.make_async_copy(prob_ref.at[heads], outs[5].at[heads], sem.at[10 + i])

    spans = key_spans(tokens, reach)
    for i in range(HEADS // 2):
        cols = slice(i * 128, i * 128 + 128)
        q2, k2 = q_ref[:, cols], k_ref[:, cols]
        kt_ref[cols, :] = (k2.astype(F32).T * SCALE).astype(BF)
        vt_ref[cols, :] = v_ref[:, cols].astype(F32).T.astype(BF)
        for half in range(2):
            span = slice(half * 64, half * 64 + 64)
            for b, (start, low, high) in enumerate(spans):
                block = slice(start, start + LANES)
                prob_ref[2 * i + half, b, : high - low] = mm_t(k2[low:high, span], q2[block, span])
    stores[3].start()
    for h in range(HEADS):
        for b, (start, low, high) in enumerate(spans):
            scores = prob_ref[h, b, : high - low] + bias_ref[low:high, start : start + LANES]
            grown = jnp.exp(scores - jnp.max(scores, axis=0, keepdims=True))
            probs = grown * (1.0 / jnp.sum(grown, axis=0, keepdims=True))
            prob_ref[h, b, : high - low] = probs
            weight_ref[h, b, : high - low] = probs.astype(BF)
        if h % 2:
            prob_store(h // 2).start()
    for h in range(HEADS):
        rows = slice(h * HEAD_DIM, (h + 1) * HEAD_DIM)
        for b, (start, low, high) in enumerate(spans):
            t_ref[rows, start : start + LANES] = mm(vt_ref[rows, :][:, low:high], weight_ref[h, b, : high - low])
    mixed_ref[...] = t_ref[...].T.astype(BF)
    stores[6].start()
    split_rows(mine_ref, other_ref, 1, t_ref, core)
    stores[0].start()
    stores[1].start()

    for i in range(HEADS // 2):
        prob_store(i).wait()
    for store in stores.values():
        store.wait()


def backward_kernel(reach, cot_ref, *rest):
    sources, blocks_ref, rest = rest[:5], rest[5], rest[6:]
    wout_ref, q_ref, kt_ref, v_ref, prob_ref, dqkv_ref, gm_ref, dqt_ref, dots_ref, grad_ref, weight_ref, sem = rest
    tokens, width = cot_ref.shape
    targets = (wout_ref, q_ref, kt_ref, v_ref, prob_ref)
    loads = [pltpu.make_async_copy(src, dst, sem.at[i]) for i, (src, dst) in enumerate(zip(sources, targets))]
    for load in loads:
        load.start()
    loads[0].wait()
    gm_ref[...] = mm_t(cot_ref[...], wout_ref[...]).astype(BF)
    for load in loads[1:]:
        load.wait()
    spans = key_spans(tokens, reach)

    for h in range(HEADS):
        cols = slice(h * HEAD_DIM, (h + 1) * HEAD_DIM)
        for b, (start, low, high) in enumerate(spans):
            dots_ref[h, b, : high - low] = mm_t(v_ref[low:high, cols], gm_ref[start : start + LANES, cols])
    for h in range(HEADS):
        for b, (start, low, high) in enumerate(spans):
            block = slice(start, start + LANES)
            probs, dots = prob_ref[h, b, : high - low], dots_ref[h, b, : high - low]
            centre = jnp.sum(probs * dots, axis=0, keepdims=True)
            for dst, value in ((grad_ref, probs * (dots - centre)), (weight_ref, probs)):
                dst[h, low:high, block] = value.astype(BF)
                if low:
                    dst[h, :low, block] = jnp.zeros((low, LANES), BF)
                if high < tokens:
                    dst[h, high:, block] = jnp.zeros((tokens - high, LANES), BF)
    for i in range(HEADS // 2):
        cols = slice(i * 128, i * 128 + 128)
        q2, g2 = q_ref[:, cols], gm_ref[:, cols]
        for at, source, right in ((1, grad_ref, q2), (2, weight_ref, g2)):
            pair = [mm(source[2 * i + half], right[:, half * 64 : half * 64 + 64]) for half in range(2)]
            dqkv_ref[:, at * width + i * 128 : at * width + i * 128 + 128] = jnp.concatenate(pair, 1).astype(BF)
        for h in (2 * i, 2 * i + 1):
            rows = slice(h * HEAD_DIM, (h + 1) * HEAD_DIM)
            dqt_ref[rows, :] = mm(kt_ref[rows, :], grad_ref[h])
    dqkv_ref[:, :width] = dqt_ref[...].T.astype(BF)
    runs = blocks_ref.shape[0]
    wide, thin = 3 * width // runs, width // runs
    for j in range(runs):
        blocks_ref[j, :, :wide] = dqkv_ref[:, j * wide : (j + 1) * wide]
        blocks_ref[j, :, wide:] = cot_ref[:, j * thin : (j + 1) * thin]


def norm_kernel(inner, x_ref, cot_ref, gain_ref, blocks_ref, wqkv_ref, mixed_ref, back_ref, dqkv_ref, extra_ref):
    tokens, width = x_ref.shape
    runs = blocks_ref.shape[0]
    wide = 3 * width // runs
    for j in range(runs):
        dqkv_ref[:, j * wide : (j + 1) * wide] = blocks_ref[j, :, :wide]
    unit, spread = row_stats(x_ref[...].astype(F32))
    ngrad = mm_t(dqkv_ref[...], wqkv_ref[...])
    part = jnp.sum(ngrad * unit, axis=0, keepdims=True)
    scaled = ngrad * gain_ref[...]
    mean_one = jnp.mean(scaled, axis=-1, keepdims=True)
    second = jnp.mean(scaled * unit, axis=-1, keepdims=True)
    back_ref[:, :width] = mixed_ref[...]
    back_ref[:, width : 2 * width] = (cot_ref[...].astype(F32) + spread * (scaled - mean_one - unit * second)).astype(BF)
    high = part.astype(BF).astype(F32)
    extra_ref[...] = jnp.zeros_like(extra_ref)
    share, each = width // inner, tokens // (runs * inner)
    for k, value in enumerate((high, part - high)):
        row, lane = k % each, k // each * LANES
        for i in range(inner):
            piece = value[:, i * share : (i + 1) * share]
            for t in range(runs):
                start = (t * inner + i) * each + row
                extra_ref[start : start + 1, lane : lane + share] = piece
    back_ref[:, 2 * width :] = extra_ref[...].astype(BF)


def finish_kernel(inv_root, frames_ref, wout_ref, back_ref, block_ref, fgrad_ref, gain_ref):
    width, share = fgrad_ref.shape[1], gain_ref.shape[1]
    block_ref[...] = (frames_ref[...].astype(F32) + mm(back_ref[:, :width], wout_ref[...])).astype(BF)
    fgrad_ref[...] = back_ref[:, width : 2 * width]
    total = jnp.sum(back_ref[:, 2 * width :].astype(F32), axis=0, keepdims=True)
    parts = [total[:, k : k + share] for k in range(0, total.shape[1], LANES)]
    gain_ref[...] = sum(parts) * inv_root


def squeeze_bits(value, bits):
    for b in sorted(bits, reverse=True):
        value = (value >> (b + 1) << b) | (value & ((1 << b) - 1))
    return value


def spread_bits(value, bits):
    for b in sorted(bits):
        value = (value >> b << (b + 1)) | (value & ((1 << b) - 1))
    return value


def bit_order(runs, part):
    bits = list(range(runs.bit_length() - 1))
    shift = part % len(bits)
    return bits[shift:] + bits[:shift]


def run_of(runs, part, stage, n):
    me = lax.axis_index("tm")
    order = bit_order(runs, part)
    past, bit = order[:stage], order[stage]
    run = spread_bits(n, past + [bit])
    for b in past:
        run = run | (me & (1 << b))
    return run | ((me ^ (1 << bit)) & (1 << bit))


def place_of(runs, part, stage, run):
    return squeeze_bits(run, bit_order(runs, part)[: stage + 1])


def exchange(values, runs, stage):
    found = []
    for part, value in enumerate(values):
        bit = bit_order(runs, part)[stage]
        found.append(lax.ppermute(value, "tm", [(t, t ^ (1 << bit)) for t in range(runs)]))
    return found


def to_partner(value, inner):
    return lax.ppermute(value, "inner", [(i, i ^ 1) for i in range(inner)])


def pieces_of(rows):
    cut = rows // 2
    return ((0, cut), (cut, rows))


def product_kernel(choose, mine_ref, other_ref, d_ref, d_other_ref, *out_refs):
    _, count, _, tokens = mine_ref.shape
    wide = d_ref.shape[2] * 3 // 4
    for out_ref, ((low, high), (first, last), runs) in zip(out_refs, choose()):
        cuts = ((0, first, min(last, wide)), (1, max(first, wide), last))
        for n, run in enumerate(runs):
            totals = []
            for slot, start, stop in cuts:
                if start < stop:
                    left = mine_ref[slot, :, low:high].reshape(count * (high - low), tokens)
                    right = other_ref[slot, :, low:high].reshape(count * (high - low), tokens)
                    totals.append(mm(left, d_ref[run, :, start:stop]) + mm(right, d_other_ref[run, :, start:stop]))
            total = jnp.concatenate(totals, 1) if len(totals) > 1 else totals[0]
            total = total.astype(out_ref.dtype)
            for z in range(count):
                out_ref[n, z] = total[z * (high - low) : (z + 1) * (high - low)]


def with_received(runs, part, run, total, got_refs, z):
    for stage, ref in enumerate(got_refs):
        total = total + ref[place_of(runs, part, stage, run), z].astype(F32)
    return total


def stage_kernel(runs, stage, final, *refs):
    own_refs, refs = refs[:PARTS], refs[PARTS:]
    if final:
        mine_ref, rest_ref, refs = refs[0], refs[-1], refs[1:-1]
    got_refs, out_refs = refs[:-PARTS], refs[-PARTS:]
    run = lax.axis_index("tm")
    for part, (own_ref, out_ref) in enumerate(zip(own_refs, out_refs)):
        for n in range(out_ref.shape[0]):
            other = run_of(runs, part, stage, n)
            for z in range(out_ref.shape[1]):
                out_ref[n, z] = with_received(runs, part, other, own_ref[n, z], got_refs[part::PARTS], z).astype(BF)
        if final:
            lanes = out_ref.shape[3]
            cols = slice(part * lanes, (part + 1) * lanes)
            for z in range(out_ref.shape[1]):
                rest_ref[0, z, :, cols] = with_received(runs, part, run, mine_ref[0, z, :, cols], got_refs[part::PARTS], z)


def first_row_kernel(mine_ref, *refs):
    got_refs, (send_ref, rest_ref) = refs[:-2], refs[-2:]
    me = lax.axis_index("inner") >> 1

    def total(z):
        return mine_ref[0, z] + jnp.concatenate([ref[0, z].astype(F32) for ref in got_refs], 1)

    for n in range(send_ref.shape[0]):
        z = spread_bits(n, [0])
        rest_ref[n] = total(z | (me & 1))
        send_ref[n] = total(z | (1 - (me & 1))).astype(BF)


def row_kernel(stage, keep_ref, got_ref, send_ref, rest_ref):
    bit = (lax.axis_index("inner") >> (stage + 1)) & 1
    for n in range(send_ref.shape[0]):
        rest_ref[n] = keep_ref[2 * n + bit] + got_ref[2 * n + bit].astype(F32)
        other = 2 * n + 1 - bit
        send_ref[n] = (keep_ref[other] + got_ref[other].astype(F32)).astype(BF)


def owners_kernel(mine_ref, *refs):
    got_refs, (own_ref, *send_refs) = refs[:PARTS], refs[PARTS:]
    count = mine_ref.shape[1]
    me = lax.axis_index("inner") >> 1

    def total(z):
        return mine_ref[0, z] + jnp.concatenate([ref[0, z].astype(F32) for ref in got_refs], 1)

    for k, ref in enumerate(send_refs):
        ref[0] = total(lax.rem(me + k + 1, count)).astype(BF)
    own_ref[0] = total(me)


def last_kernel(inv_root, sizes, *rest):
    parts, (q_ref, o_ref) = rest[:-2], rest[-2:]
    wide = q_ref.shape[1]
    for size, (low, high) in zip(sizes, pieces_of(q_ref.shape[0])):
        (own_ref, *others), parts = parts[:size], parts[size:]
        total = own_ref[0]
        for ref in others:
            total = total + ref[0].astype(F32)
        total = total * inv_root
        q_ref[low:high] = total[:, :wide]
        o_ref[low:high] = total[:, wide:]


def reduce_weights(mine, other, d, d_other, runs, inner, inv_root):
    sds = jax.ShapeDtypeStruct
    _, count, rows, tokens = mine.shape
    lanes = d.shape[2]
    stages = runs.bit_length() - 1
    pieces = pieces_of(rows)
    args = (mine, other, d, d_other)

    each = lanes // PARTS

    def block(piece, part, stage):
        if part is None:
            return piece, (0, lanes), [lax.axis_index("tm")]
        return piece, (part * each, (part + 1) * each), [run_of(runs, part, stage, n) for n in range(runs >> (stage + 1))]

    def shape_of(piece, part, stage):
        (low, high), wide = piece, lanes if part is None else each
        return (1 if part is None else runs >> (stage + 1), count, high - low, wide)

    def product(wanted, dtype):
        shapes = [shape_of(*each) for each in wanted]
        flops = sum(4 * math.prod(shape) * tokens for shape in shapes)
        body = functools.partial(product_kernel, lambda: [block(*each) for each in wanted])
        near = range(len(shapes)) if dtype == BF else ()
        return call(body, tuple(sds(shape, dtype) for shape in shapes), *args, flops=flops, near_in=range(4), near_out=near, far_out=dtype == F32)

    got = [[] for _ in pieces]
    for p, piece in enumerate(pieces):
        sends = product([(piece, part, 0) for part in range(PARTS)], BF)
        got[p].append(exchange(sends, runs, 0))
    wanted = [(piece, part, stage) for piece in pieces for stage in range(1, stages) for part in range(PARTS)]
    wanted += [(piece, None, stages) for piece in pieces]
    later = list(product(wanted, F32))
    own = [[[later.pop(0) for _ in range(PARTS)] for _ in range(1, stages)] for _ in pieces]
    keep = later
    for stage in range(1, stages):
        final = stage == stages - 1
        for p in range(len(pieces)):
            now = own[p][stage - 1]
            out = [sds(array.shape, BF) for array in now] + ([sds(keep[p].shape, F32)] if final else [])
            held = [keep[p]] if final else []
            received = [array for arrays in got[p] for array in arrays]
            sends = call(functools.partial(stage_kernel, runs, stage, final), tuple(out), *now, *held, *received)
            if final:
                keep[p], got[p] = sends[-1], []
            got[p].append(exchange(sends[:PARTS], runs, stage))
    got = [arrays[-1] for arrays in got]
    for stage in range(count.bit_length() - 1):
        perm = [(i, i ^ (2 << stage)) for i in range(inner)]
        for p, (low, high) in enumerate(pieces):
            shape = (count >> (stage + 1), high - low, lanes)
            if p >= DIRECT_FROM and count <= 4:
                if stage == 0:
                    owned = (1, high - low, lanes)
                    out = (sds(owned, F32),) + (sds(owned, BF),) * (count - 1)
                    keep[p], *sends = call(owners_kernel, out, keep[p], *got[p])
                    got[p] = []
                    for k, send in enumerate(sends):
                        got[p].append(lax.ppermute(send, "inner", [(i, (i + 2 * (k + 1)) % inner) for i in range(inner)]))
                continue
            body = functools.partial(row_kernel, stage) if stage else first_row_kernel
            send, keep[p] = call(body, (sds(shape, BF), sds(shape, F32)), keep[p], *got[p])
            got[p] = [lax.ppermute(send, "inner", perm)]
    last = []
    for p in range(len(pieces)):
        last += [keep[p], *got[p]]
    out = (sds((rows, lanes * 3 // 4), F32), sds((rows, lanes // 4), F32))
    return call(functools.partial(last_kernel, inv_root, tuple(1 + len(arrays) for arrays in got)), out, *last)


def to_tubes(rows, count):
    held, patches, width = rows.shape
    parts = jnp.moveaxis(rows.reshape(held, count, patches // count, width), 1, 0)
    parts = lax.all_to_all(parts, AXES, split_axis=0, concat_axis=0, tiled=True)
    return parts.reshape(-1, width)


def to_frames(tubes, count, held, patches):
    width = tubes.shape[1]
    parts = tubes.reshape(count, held, patches // count, width)
    parts = lax.all_to_all(parts, AXES, split_axis=0, concat_axis=0, tiled=True)
    return jnp.moveaxis(parts, 0, 1).reshape(held, patches, width)


def window_bias(all_frames, patches, clip_len):
    tokens = all_frames * patches
    key = lax.broadcasted_iota(jnp.int32, (tokens, tokens), 0)
    query = lax.broadcasted_iota(jnp.int32, (tokens, tokens), 1)
    key_f, query_f = key // patches, query // patches
    inside = (key % patches == query % patches) & (abs(key_f - query_f) <= WINDOW)
    inside = inside & (key_f // clip_len == query_f // clip_len)
    return jnp.where(inside, 0.0, -1e30).astype(F32)


def attend(x, gain, w_qkv, bias, reach, inner):
    tokens, width = x.shape
    spans = key_spans(tokens, reach)
    longest = max(high - low for _, low, high in spans)
    sds, vmem = jax.ShapeDtypeStruct, pltpu.VMEM
    halves = ((2, inner // 2, width // inner, tokens), BF)
    flat, turned = ((tokens, width), BF), ((width, tokens), BF)
    probs = ((HEADS, len(spans), longest, LANES), F32)
    made = (halves, halves, flat, turned, flat, probs, flat)
    return call(
        functools.partial(forward_kernel, reach),
        tuple(sds(*each) for each in made),
        x,
        gain,
        bias,
        w_qkv,
        scratch=[vmem((3, width, width), BF), *(vmem(*each) for each in made), vmem(*flat), vmem(*flat), vmem(*turned), vmem((width, tokens), F32), vmem(probs[0], BF)],
        flops=2 * tokens * width * 4 * width,
        raw_in=(3,),
        raw_out=range(7),
        copies=10 + HEADS // 2,
    )


def attend_back(cot, w_out, q, kt, v, prob, reach, runs):
    tokens, width = cot.shape
    sds, vmem = jax.ShapeDtypeStruct, pltpu.VMEM
    flat, turned, probs = (q.shape, BF), (kt.shape, BF), (prob.shape, F32)
    made = ((runs, tokens, 4 * width // runs), BF)
    return call(
        functools.partial(backward_kernel, reach),
        sds(*made),
        cot,
        w_out,
        q,
        kt,
        v,
        prob,
        scratch=[*(vmem(*each) for each in (((width, width), BF), flat, turned, flat, probs)), vmem((tokens, 3 * width), BF), vmem(*flat), vmem((width, tokens), F32), vmem(*probs), vmem((HEADS, tokens, tokens), BF), vmem((HEADS, tokens, tokens), BF)],
        flops=2 * tokens * width * 4 * width,
        raw_in=range(1, 6),
        copies=5,
    )


def shards(frames, norm_gain, w_qkv, w_out, cotangent):
    held, patches, width = frames.shape
    runs, inner = lax.axis_size("tm"), lax.axis_size("inner")
    count = runs * inner
    all_frames = held * count
    clip_len = min(CLIP_MAX, all_frames)
    inv_root = 1.0 / math.sqrt(all_frames * patches)
    tokens = all_frames * patches // count
    reach = WINDOW * (patches // count)
    gain = norm_gain.reshape(1, width)
    bias = window_bias(all_frames, patches // count, clip_len)
    spans = key_spans(tokens, reach)
    longest = max(high - low for _, low, high in spans)
    sds = jax.ShapeDtypeStruct
    vmem = pltpu.VMEM

    x = to_tubes(frames, count)
    cot = to_tubes(cotangent, count)
    mine, other, q, kt, v, prob, mixed = attend(x, gain, w_qkv, bias, reach, inner)
    theirs = to_partner(other, inner)
    blocks = attend_back(cot, w_out, q, kt, v, prob, reach, runs)
    blocks_other = to_partner(blocks, inner)
    extra = -(-2 // (tokens // count)) * LANES
    back = call(
        functools.partial(norm_kernel, inner),
        sds((tokens, 2 * width + extra), BF),
        x,
        cot,
        gain,
        blocks,
        w_qkv,
        mixed,
        scratch=[vmem((tokens, 3 * width), BF), vmem((tokens, extra), F32)],
        flops=2 * tokens * width * 3 * width,
    )
    back = to_frames(back, count, held, patches).reshape(held * patches, -1)
    owned = sds((held * patches, width), BF)
    block_out, frames_grad, gain_grad = call(
        functools.partial(finish_kernel, inv_root),
        (owned, owned, sds((1, width // inner), F32)),
        frames.reshape(-1, width),
        w_out,
        back,
        flops=2 * tokens * width * width,
    )
    block_out, frames_grad = block_out.reshape(frames.shape), frames_grad.reshape(frames.shape)
    qkv_grad, out_grad = reduce_weights(mine, theirs, blocks, blocks_other, runs, inner, inv_root)
    return block_out, frames_grad, qkv_grad, out_grad, gain_grad.reshape(-1)


def solution(mesh):
    in_specs = (P(AXES, None, None), P(), P(), P(), P(AXES, None, None))
    out_specs = (P(AXES, None, None), P(AXES, None, None), P("inner", "tm"), P("inner", "tm"), P("inner"))
    return jax.shard_map(shards, mesh=mesh, in_specs=in_specs, out_specs=out_specs, check_vma=False)
```
